32 devices in a mesh: tp: 2 (over core), ep: 16 (over z, y, x).
Axes of the slice: x: 2, y: 2, z: 4, core: 2. Of those that a mesh axis runs over, the one named last changes fastest.
Arguments:
- tokens: bfloat16 [2048, 4096], P('ep', 'tp'), may hold values from -6 to 6
- expert_ids: int32 [2048, 8], P('ep'), may hold values from 0 to 15, all different within a row; in each aligned block of 128 rows (0 to 127, 128 to 255, ...) at most 128 rows name the same one
- route_weights: float32 [2048, 8], P('ep'), may hold values from 0.1 to 1
- gate_weight: bfloat16 [16, 4096, 1536], P('ep', None, 'tp'), may hold values from -0.09375 to 0.09375
- up_weight: bfloat16 [16, 4096, 1536], P('ep', None, 'tp'), may hold values from -0.09375 to 0.09375
- down_weight: bfloat16 [16, 1536, 4096], P('ep', 'tp'), may hold values from -0.15625 to 0.15625
- value_weight: float32 [4096], P('tp'), may hold values from -0.375 to 0.375
- sequence_ids: int32 [16, 128], P('ep'), may hold values from 0 to 3, never falling along the last dimension, each value on 1 to 64 neighbouring positions
Outputs:
- layer_output: bfloat16 [2048, 4096], P('ep', 'tp')
- rewards: float32 [16, 4], P('ep')
The draws below stay inside these ranges and needn't reach their ends.
Inputs may be any that keep to these rules, and one draw needn't show every extreme that they name: `expert_ids`: each token names 8 different experts. Within each group's 128 rows no expert is named more than 128 times, a bound that some block reaches. `sequence_ids`: within each group the ids never fall, every one of the 4 ids occurs, and the longest sequence has exactly 64 tokens.
All inputs are finite; a program needn't handle non-finite values.
Results may differ from the reference program's by a relative error of at most 0.0095.
Values may be sent and summed in bfloat16 or wider, within the bound.
A program may use at most 128 MiB of HBM per device.

```python
import math
import jax
import jax.numpy as jnp
import numpy as np
from jax import lax

D = 4096
FF = 1536
TOP = 8
TOK_GRP = 128
SEQ_GRP = 4
GROUPS = 16
EXPERTS = 16
CAP = 128
TOKENS = 2048
N_TP = 2


def block_levels(own_key, dims, cuts, least, top_value):
    def one(dim, parts):
        heights = jax.random.uniform(jax.random.fold_in(jax.random.fold_in(own_key, 6), dim), (parts,), jnp.float32, least / len(cuts), top_value / len(cuts))
        return jnp.repeat(jnp.exp(heights), dims[dim] // parts).reshape((-1,) + (1,) * (len(dims) - dim - 1))

    factor_of = one(*cuts[0])
    for cut in cuts[1:]:
        factor_of = factor_of * one(*cut)
    return factor_of


def length_profile(count, total, most, slope):
    portions = [(1 << 20) // math.isqrt(standing ** slope) + 1 for standing in range(2, count + 1)]
    surplus, given = total - most - (count - 1), [1] * (count - 1)
    while surplus > 0:
        free = [i for i in range(count - 1) if given[i] < most]
        mass, budget = sum([portions[i] for i in free]), surplus
        for i in free:
            addition = min(most - given[i], max(1, budget * portions[i] // mass), surplus)
            given[i] = given[i] + addition
            surplus = surplus - addition
    return np.array([most] + given)


def ragged_sizes(own_key, number_of, total, most, lean):
    if number_of == 2:
        one = jax.random.randint(own_key, (), max(1, total - most), min(most, total - 1) + 1)
        return jnp.stack([one, total - one])
    lengths = jnp.asarray(length_profile(number_of, total, most, lean), jnp.int32)
    pairs = (number_of - 1) // 2
    giver, receiver = lengths[1:1 + 2 * pairs:2], lengths[2:2 + 2 * pairs:2]
    room = jnp.minimum(giver - 1, most - receiver)
    moved = jax.random.randint(jax.random.fold_in(own_key, 1), (pairs,), 0, 1 << 20) % (room + 1)
    lengths = lengths.at[1:1 + 2 * pairs:2].set(giver - moved).at[2:2 + 2 * pairs:2].set(receiver + moved)
    return lengths[jax.random.permutation(jax.random.fold_in(own_key, 2), number_of)]


def routed_block(key, own, number, rows, count, top, bound, lean):
    sequence = jax.random.permutation(key, count)
    heavy_load, usual = shares(count, rows * top, bound, lean, True), shares(count, rows * top, bound, lean, False)
    places = jnp.arange(count)

    def named(tallies, turn):
        used = int((tallies > 0).sum())
        fixed = max(1, used // 4)
        passed = fixed + (places - fixed + turn * (used - fixed)) % max(1, count - fixed)
        return jnp.zeros((count,), jnp.int32).at[sequence[jnp.where(places < fixed, places, passed)]].set(jnp.asarray(tallies, jnp.int32))

    tallies = jnp.where(number % 4 == 0, named(heavy_load, number // 4), named(usual, number - number // 4 - 1))
    mixed = jax.random.permutation(jax.random.fold_in(own, 3), count)
    donor, receiver = mixed[0:count // 2 * 2:2], mixed[1:count // 2 * 2:2]
    slack = jnp.minimum(tallies[donor] - 1, bound - tallies[receiver]) // 2
    slack = jnp.where((donor == sequence[0]) | (receiver == sequence[0]) | (tallies[receiver] == 0), 0, jnp.maximum(slack, 0))
    passed = jax.random.randint(jax.random.fold_in(own, 4), (count // 2,), 0, 1 << 20) % (slack + 1)
    tallies = tallies.at[donor].add(-passed).at[receiver].add(passed)
    labels = jnp.searchsorted(jnp.cumsum(tallies), jnp.arange(rows * top), side="right").astype(jnp.int32)
    grid = labels.reshape(top, rows).T
    grid = grid[jax.random.permutation(jax.random.fold_in(own, 1), rows)]
    turn = jax.random.randint(jax.random.fold_in(own, 2), (rows, 1), 0, top)
    return jnp.take_along_axis(grid, (jnp.arange(top)[None, :] + turn) % top, axis=1)


def shares(number_of, total, most, slope, full):
    loads = [(1 << 20) // math.isqrt(grade ** slope) + 1 for grade in range(1, number_of + 1)]
    largest = most if full else min(most, max(-(-total // number_of), total * loads[0] // sum(loads)))
    least = 1 if total - largest >= number_of - 1 else 0
    holding, rest = [largest] + [least] * (number_of - 1), total - largest - least * (number_of - 1)
    while rest > 0:
        movable = [i for i in range(1, number_of) if holding[i] < largest] or [i for i in range(1, number_of) if holding[i] < most]
        pool, budget = sum([loads[i] for i in movable]), rest
        for i in movable:
            addition = min(most - holding[i], max(1, budget * loads[i] // pool), rest)
            holding[i] = holding[i] + addition
            rest = rest - addition
    return np.array(holding)


def noise(stream_key, shape, width, most, cuts=(), kind=jnp.bfloat16):
    array = width * jax.random.normal(stream_key, shape, jnp.float32)
    if cuts:
        array = array * block_levels(stream_key, shape, cuts, -0.22, 0.18)
    return jnp.clip(array, -most, most).astype(kind)


def setup_inputs(seed: int = 0) -> dict:
    key_list = jax.random.split(jax.random.key(seed), 9)
    tokens = noise(key_list[0], (TOKENS, D), 1.0, 6.0, ((0, 16), (1, 2)))
    expert_ids_keys = jax.random.split(jax.random.fold_in(key_list[1], 1), TOKENS // TOK_GRP)
    expert_ids_turns = jax.random.permutation(jax.random.fold_in(key_list[1], 3), TOKENS // TOK_GRP)
    expert_ids = jax.vmap(lambda own, number: routed_block(jax.random.fold_in(key_list[1], 2), own, number, TOK_GRP, EXPERTS, TOP, CAP, 2))(expert_ids_keys, expert_ids_turns).reshape((TOKENS, TOP))
    route_weights = jnp.clip(jnp.exp(math.log(1.0) - 2.3025851 * jax.random.uniform(key_list[2], (TOKENS, TOP), jnp.float32) ** block_levels(key_list[2], (TOKENS, TOP), ((0, 16),), -0.2, 0.2)), 0.1, 1.0)
    gate_weight = noise(key_list[3], (EXPERTS, D, FF), D ** -0.5, 0.09375, ((0, 16), (2, 2)))
    up_weight = noise(key_list[4], (EXPERTS, D, FF), D ** -0.5, 0.09375, ((0, 16), (2, 2)))
    down_weight = noise(key_list[5], (EXPERTS, FF, D), FF ** -0.5, 0.15625, ((0, 16), (1, 2)))
    value_weight = noise(key_list[6], (D,), (D // 16) ** -0.5, 0.375, ((0, 2),), jnp.float32)
    sequence_ids = jax.vmap(lambda own: jnp.searchsorted(jnp.cumsum(ragged_sizes(own, SEQ_GRP, TOK_GRP, TOK_GRP // 2, 0)), jnp.arange(TOK_GRP), side="right"))(jax.random.split(key_list[7], GROUPS)).reshape((GROUPS, TOK_GRP)).astype(jnp.int32)
    return {"tokens": tokens, "expert_ids": expert_ids, "route_weights": route_weights, "gate_weight": gate_weight, "up_weight": up_weight, "down_weight": down_weight, "value_weight": value_weight, "sequence_ids": sequence_ids}


def slot_tables(route_ids, experts, capacity):
    tok_count, top_count = route_ids.shape
    flat_ids = route_ids.reshape(tok_count * top_count).astype(jnp.int32)
    one_hot = (flat_ids[:, None] == jnp.arange(experts, dtype=jnp.int32)[None, :]).astype(jnp.int32)
    before = jnp.cumsum(one_hot, axis=0, dtype=jnp.int32) - one_hot
    position = lax.optimization_barrier(jnp.sum(before * one_hot, axis=1, dtype=jnp.int32))
    slot_index = (flat_ids * capacity + position).astype(jnp.int32)
    pair_token = (jnp.arange(tok_count * top_count, dtype=jnp.int32) // top_count).astype(jnp.int32)
    owner_token = jnp.zeros((experts * capacity,), jnp.int32).at[slot_index].set(pair_token)
    filled = jnp.zeros((experts * capacity,), jnp.int32).at[slot_index].set(1)
    return (slot_index.reshape(tok_count, top_count), owner_token, filled)

def expert_apply(operands):
    rows_in, gate_mat, up_mat, down_mat = operands
    gate = jnp.dot(rows_in, gate_mat, preferred_element_type=jnp.float32)
    upper = jnp.dot(rows_in, up_mat, preferred_element_type=jnp.float32)
    hidden = (jax.nn.silu(gate) * upper).astype(jnp.bfloat16)
    quarter = FF // N_TP
    total = jnp.zeros((rows_in.shape[0], D), jnp.float32)
    for index in range(N_TP):
        part_sum = jnp.dot(hidden[:, index * quarter:(index + 1) * quarter], down_mat[index * quarter:(index + 1) * quarter], preferred_element_type=jnp.float32)
        total = total + part_sum.astype(jnp.bfloat16).astype(jnp.float32)
    return total.astype(jnp.bfloat16)

def reference(tokens, expert_ids, route_weights, gate_weight, up_weight, down_weight, value_weight, sequence_ids):
    ids_grouped = expert_ids.reshape(GROUPS, TOK_GRP, TOP)
    slot_index, owner_token, filled = jax.vmap(lambda ids: slot_tables(ids, EXPERTS, CAP))(ids_grouped)
    token_blocks = tokens.reshape(GROUPS, TOK_GRP, D)

    def build(block, owners, live):
        return block[owners] * live.astype(jnp.bfloat16)[:, None]
    outgoing = jax.vmap(build)(token_blocks, owner_token, filled)
    per_expert = outgoing.reshape(GROUPS, EXPERTS, CAP, D).transpose(1, 0, 2, 3).reshape(EXPERTS, GROUPS * CAP, D)
    results = lax.map(expert_apply, (per_expert, gate_weight, up_weight, down_weight))
    back_rows = results.reshape(EXPERTS, GROUPS, CAP, D).transpose(1, 0, 2, 3).reshape(GROUPS, EXPERTS * CAP, D)
    picked = jax.vmap(lambda rows_back, slots: rows_back[slots])(back_rows, slot_index)
    weights_grouped = route_weights.reshape(GROUPS, TOK_GRP, TOP).astype(jnp.float32)
    share = weights_grouped / lax.optimization_barrier(jnp.sum(weights_grouped, axis=2, keepdims=True))
    combined = token_blocks.astype(jnp.float32) + jnp.einsum('gtk,gtkd->gtd', share, picked.astype(jnp.float32))
    layer_output = combined.astype(jnp.bfloat16)
    as_float = layer_output.astype(jnp.float32)
    squares = lax.optimization_barrier(jnp.sum(as_float * as_float, axis=2))
    along = lax.optimization_barrier(jnp.sum(as_float * value_weight.astype(jnp.float32)[None, None, :], axis=2))
    values = along * lax.rsqrt(squares / D + 1e-06)
    members = (sequence_ids[:, None, :] == jnp.arange(SEQ_GRP, dtype=jnp.int32)[None, :, None]).astype(jnp.float32)
    sums = lax.optimization_barrier(jnp.sum(members * values[:, None, :], axis=2))
    counts = lax.optimization_barrier(jnp.sum(members, axis=2))
    rewards = sums / counts
    return (layer_output.reshape(TOKENS, D), rewards)
```

```python
import functools

import jax
import jax.numpy as jnp
from jax import lax
from jax.experimental import pallas as pl
from jax.experimental.pallas import tpu as pltpu
from jax.sharding import PartitionSpec as P

SEQ_GRP = 4
CHUNKS = 1


def head(layer_output, value_weight, sequence_ids, parts):
    width_part = layer_output.shape[1]
    as_float = layer_output.astype(jnp.float32)
    squares = jnp.sum(as_float * as_float, axis=1)
    along = jnp.sum(as_float * value_weight[None, :], axis=1)
    squares, along = lax.psum((squares, along), "tp")
    values = along * lax.rsqrt(squares / (width_part * parts) + 1e-06)
    members = (sequence_ids[0][None, :] == jnp.arange(SEQ_GRP, dtype=jnp.int32)[:, None]).astype(
        jnp.float32
    )
    sums = jnp.sum(members * values[None, :], axis=1)
    counts = jnp.sum(members, axis=1)
    rewards = sums / counts
    return rewards[None, :]


def plain_shards(
    tokens,
    expert_ids,
    route_weights,
    gate_weight,
    up_weight,
    down_weight,
    value_weight,
    sequence_ids,
):
    tok_count, width_part = tokens.shape
    groups = lax.axis_size("ep")
    parts = lax.axis_size("tp")
    share = route_weights / jnp.sum(route_weights, axis=1, keepdims=True)
    named = expert_ids[:, :, None] == jnp.arange(groups, dtype=jnp.int32)[None, None, :]
    dense = jnp.sum(jnp.where(named, share[:, :, None], 0.0), axis=1)
    dense_all = lax.all_gather(dense, "ep", axis=0)
    mine = lax.dynamic_index_in_dim(dense_all, lax.axis_index("ep"), 2, keepdims=False)
    gate_local = gate_weight[0].reshape(parts, width_part, -1)
    up_local = up_weight[0].reshape(parts, width_part, -1)
    rows = tok_count // CHUNKS
    pieces = []
    for c in range(CHUNKS):
        own = tokens[c * rows:(c + 1) * rows]
        half = lax.all_gather(own, "ep", axis=0, tiled=True)
        full = lax.all_gather(half, "tp", axis=0)
        gate = jnp.einsum("qtd,qdf->tf", full, gate_local, preferred_element_type=jnp.float32)
        upper = jnp.einsum("qtd,qdf->tf", full, up_local, preferred_element_type=jnp.float32)
        scale = mine[:, c * rows:(c + 1) * rows].reshape(groups * rows, 1)
        hidden = (jax.nn.silu(gate) * upper).astype(jnp.bfloat16)
        terms = jnp.dot(hidden, down_weight[0], preferred_element_type=jnp.float32)
        terms = (terms * scale).astype(jnp.bfloat16)
        summed = lax.psum_scatter(terms, "tp", scatter_dimension=1, tiled=True)
        pieces.append(lax.psum_scatter(summed, "ep", scatter_dimension=0, tiled=True))
    routed = jnp.concatenate(pieces, axis=0).astype(jnp.float32)
    layer_output = (tokens.astype(jnp.float32) + routed).astype(jnp.bfloat16)
    return (layer_output, head(layer_output, value_weight, sequence_ids, parts))


MESH = pl.DeviceIdType.MESH
GRP = 128
PAD = 128
ROWS = 16
STRIDE = 2
PLAN = (
    ("fgo", -1, 0.0), ("own", 0, 1.0), ("hop1", 1, 2.0), ("hop2", 2, 2.1), ("hop3", 3, 2.2),
    ("sar", 4, 4.0), ("hid", 5, 5.0), ("oth", 5, 5.2), ("mine", 6, 6.0), ("ra", 8, 7.0),
    ("cs0", 8, 7.5), ("cs1", 9, 7.55), ("cs2", 10, 7.6), ("end", 11, 7.7), ("fin", 12, 9.0),
)
ORDER = (3, 0, 2, 1)


def fused(
    tok_hbm, ids, weights, value_row, seq, gate_hbm, up_hbm, down_hbm, out, rewards,
    held, gate_w, up_w, down_w, hid, scale, part, s_in, u_in, d_in, f_in, stats, marks,
    w_sem, tok_sem, af_s, af_r, au_s, au_r, ad_s, ad_r, as_s, as_r, at_s, at_r,
    sw_s, sw_r, rs_s, rs_r, ru_s, ru_r, rd_s, rd_r, rf_s, rf_r, v_sem,
):
    f32, bf16 = jnp.float32, jnp.bfloat16
    half = out.shape[1]
    chunks = GRP // ROWS
    block = 16 * ROWS
    t = lax.axis_index("tp")
    e = lax.axis_index("ep")
    x = lax.rem(e, 2)
    y = lax.rem(lax.div(e, 2), 2)
    z = lax.div(e, 4)
    e_x = e + 1 - 2 * x
    e_y = e + 2 - 4 * y
    near = (t, e_x * (1 - t) + e_y * t)
    far = (t, e_y * (1 - t) + e_x * t)
    twin = (1 - t, e)
    above = (t, lax.rem(e + 4, 16))
    below = (t, lax.rem(e + 12, 16))
    feats = pl.ds(0, half)

    def remote(src, dst, send, recv, target):
        return pltpu.make_async_remote_copy(
            src_ref=src, dst_ref=dst, send_sem=send, recv_sem=recv,
            device_id=target, device_id_type=MESH,
        )

    def arrived(ref, sem):
        remote(ref, ref, v_sem.at[0], sem, twin).wait_recv()

    def left(ref, sem):
        remote(ref, ref, sem, v_sem.at[1], twin).wait_send()

    load_tok = pltpu.make_async_copy(tok_hbm, held.at[t, :, 0, z, 0, :, feats], tok_sem)
    load_tok.start()
    barrier = pltpu.get_barrier_semaphore()
    for target in (above, below, near, far, twin):
        pl.semaphore_signal(barrier, inc=1, device_id=target, device_id_type=MESH)
    loads = [
        pltpu.make_async_copy(a, b, w_sem.at[i])
        for i, (a, b) in enumerate(((gate_hbm, gate_w), (up_hbm, up_w), (down_hbm, down_w)))
    ]
    for load in loads:
        load.start()

    lane = lax.broadcasted_iota(jnp.int32, (GRP, PAD), 1)
    share = weights[...] / jnp.sum(weights[...], axis=1, keepdims=True)
    dense = jnp.zeros((GRP, PAD), f32)
    for k in range(ids.shape[1]):
        dense += jnp.where(lax.rem(lane, 16) == ids[:, k:k + 1], share[:, k:k + 1], 0.0)
    top = dense.astype(bf16).astype(f32)
    middle = (dense - top).astype(bf16).astype(f32)
    low = dense - top - middle
    pieces = jnp.where(lane < 16, top, jnp.where(lane < 32, middle, jnp.where(lane < 48, low, 0.0)))
    pieces = pieces.astype(bf16)
    for c in range(chunks):
        held[t, c, 0, z, 0, :, pl.ds(half, PAD)] = pieces[c * ROWS:(c + 1) * ROWS]
    marks[...] = jnp.transpose(jnp.broadcast_to(seq[...].astype(f32), (GRP, PAD)))
    load_tok.wait()
    pl.semaphore_wait(barrier, 5)

    def pair(c, d):
        return held.at[t, c, 0, d]

    def fgo(c):
        remote(
            held.at[t, c, 0, z, 0], held.at[t, c, 0, z, 1], af_s.at[0], af_r.at[c], near
        ).start()

    def up_go(c, k):
        remote(pair(c, z - k), pair(c, z - k), au_s.at[0], au_r.at[c, k], above).start()

    def down_go(c, k):
        remote(pair(c, z + k), pair(c, z + k), ad_s.at[0], ad_r.at[c, k], below).start()

    def far_go(c, d):
        remote(pair(c, d), held.at[t, c, 1, d], as_s.at[0], as_r.at[c, d], far).start()

    def twin_go(c, s):
        for f in range(2):
            remote(
                held.at[t, c, s, :, f], held.at[t, c, f, :, s], at_s.at[0], at_r.at[c], twin
            ).start()

    def own(c):
        arrived(held.at[t, c, 0, z, 1], af_r.at[c])
        pl.when(z < 3)(lambda: up_go(c, 0))
        pl.when(z > 0)(lambda: down_go(c, 0))
        far_go(c, z)

    def hop(k, c):
        def from_below():
            arrived(pair(c, z - k), au_r.at[c, k - 1])
            if k < 3:
                pl.when(z < 3)(lambda: up_go(c, k))
            far_go(c, z - k)

        def from_above():
            arrived(pair(c, z + k), ad_r.at[c, k - 1])
            if k < 3:
                pl.when(z > 0)(lambda: down_go(c, k))
            far_go(c, z + k)

        pl.when(z >= k)(from_below)
        pl.when(z + k <= 3)(from_above)
        if k == 3:
            twin_go(c, 0)

    def sar(c):
        for d in range(4):
            arrived(held.at[t, c, 1, d], as_r.at[c, d])
        twin_go(c, 1)

    def flat(value):
        return value.reshape(block, value.shape[-1])

    def hidden(c):
        if c == 0:
            for load in loads:
                load.wait()
        arrived(held.at[1 - t, c], at_r.at[c])
        lanes = lax.broadcasted_iota(jnp.int32, (block, PAD), 1)
        shares = flat(held[t, c, :, :, :, :, pl.ds(half, PAD)]).astype(f32)
        scale[...] = jnp.sum(jnp.where(lax.rem(lanes, 16) == e, shares, 0.0), axis=1, keepdims=True)
        a = flat(held[0, c, :, :, :, :, feats])
        b = flat(held[1, c, :, :, :, :, feats])
        g = jnp.dot(a, gate_w[pl.ds(0, half)], preferred_element_type=f32)
        g += jnp.dot(b, gate_w[pl.ds(half, half)], preferred_element_type=f32)
        u = jnp.dot(a, up_w[pl.ds(0, half)], preferred_element_type=f32)
        u += jnp.dot(b, up_w[pl.ds(half, half)], preferred_element_type=f32)
        hid[...] = (g / (1.0 + jnp.exp(-g)) * u * scale[...]).astype(bf16)

    def term(n, core):
        cols = pl.ds(pl.multiple_of(core * half + n * 512, 512), 512)
        return jnp.dot(hid[...], down_w[:, cols], preferred_element_type=f32)

    def other(c):
        def step(n, carry):
            cols = pl.ds(pl.multiple_of(n * 512, 512), 512)
            value = term(n, 1 - t).astype(bf16)
            held[1 - t, c, :, :, :, :, cols] = value.reshape(2, 4, 2, ROWS, 512)
            return carry

        lax.fori_loop(0, half // 512, step, 0)
        for s in range(2):
            for f in range(2):
                remote(
                    held.at[1 - t, c, s, :, f, :, feats], part.at[c, f, :, s],
                    sw_s.at[0], sw_r.at[c], twin,
                ).start()

    def mine(c):
        arrived(part.at[c], sw_r.at[c])

        def step(n, carry):
            cols = pl.ds(pl.multiple_of(n * 512, 512), 512)
            total = term(n, t) + flat(part[c, :, :, :, :, cols]).astype(f32)
            part[c, :, :, :, :, cols] = total.astype(bf16).reshape(2, 4, 2, ROWS, 512)
            return carry

        lax.fori_loop(0, half // 512, step, 0)
        for d in ORDER:
            remote(part.at[c, 1, d], s_in.at[c, d], rs_s.at[0], rs_r.at[c, d], far).start()

    def add(dst, src):
        for f in range(2):
            dst[f] = dst[f] + src[f]

    def ra(c):
        for d in ORDER:
            arrived(s_in.at[c, d], rs_r.at[c, d])
            add(part.at[c, 0, d], s_in.at[c, d])

    def cs(h, c):
        def up():
            for d in range(3, h, -1):
                if h > 0:
                    arrived(u_in.at[c, d - 1], ru_r.at[c, d - 1])
                    add(part.at[c, 0, d], u_in.at[c, d - 1])
                remote(
                    part.at[c, 0, d], u_in.at[c, d - 1], ru_s.at[0], ru_r.at[c, d - 1], above
                ).start()

        def down():
            for d in range(3 - h):
                if h > 0:
                    arrived(d_in.at[c, d], rd_r.at[c, d])
                    add(part.at[c, 0, d], d_in.at[c, d])
                remote(
                    part.at[c, 0, d], d_in.at[c, d], rd_s.at[0], rd_r.at[c, d], below
                ).start()

        pl.when(z == h)(up)
        pl.when(z == 3 - h)(down)

    def end(c):
        def from_below():
            arrived(u_in.at[c, z - 1], ru_r.at[c, z - 1])
            add(part.at[c, 0, z], u_in.at[c, z - 1])

        def from_above():
            arrived(d_in.at[c, z], rd_r.at[c, z])
            add(part.at[c, 0, z], d_in.at[c, z])

        pl.when(z > 0)(from_below)
        pl.when(z < 3)(from_above)
        remote(part.at[c, 0, z, 1], f_in.at[c], rf_s.at[0], rf_r.at[c], near).start()

    def fin(c):
        arrived(f_in.at[c], rf_r.at[c])
        total = part[c, 0, z, 0].astype(f32) + f_in[c].astype(f32)
        total += held[t, c, 0, z, 0, :, feats].astype(f32)
        rounded = total.astype(bf16)
        rows = pl.ds(c * ROWS, ROWS)
        out[rows] = rounded
        as_float = rounded.astype(f32)
        squares = jnp.sum(as_float * as_float, axis=1, keepdims=True)
        along = jnp.sum(as_float * value_row[...], axis=1, keepdims=True)
        lanes = lax.broadcasted_iota(jnp.int32, (ROWS, PAD), 1)
        stats[0, rows] = jnp.where(lanes == 0, squares, along)

    steps = {
        "fgo": fgo, "own": own, "sar": sar, "hid": hidden, "oth": other, "mine": mine, "ra": ra,
        "end": end, "fin": fin,
    }
    for k in (1, 2, 3):
        steps["hop%d" % k] = functools.partial(hop, k)
        steps["cs%d" % (k - 1)] = functools.partial(cs, k - 1)
    turns = [
        (STRIDE * c + slot, place, c, name) for c in range(chunks) for name, slot, place in PLAN
    ]
    for _, _, c, name in sorted(turns):
        steps[name](c)

    trade = remote(stats.at[0], stats.at[1], v_sem.at[0], v_sem.at[1], twin)
    trade.start()
    left(held.at[t, :, 0, 0, 0], af_s.at[0])
    left(held.at[t, :, 0], as_s.at[0])
    left(held.at[t], at_s.at[0])
    left(part, sw_s.at[0])
    left(part.at[:, 1], rs_s.at[0])
    left(part.at[:, 0, 0, 0], rf_s.at[0])
    for k in range(4):
        def line(k=k):
            if k < 3:
                left(held.at[t, :, 0, pl.ds(0, k + 1)], au_s.at[0])
                left(part.at[:, 0, pl.ds(0, 3 - k)], ru_s.at[0])
            if k > 0:
                left(held.at[t, :, 0, pl.ds(0, 4 - k)], ad_s.at[0])
                left(part.at[:, 0, pl.ds(0, k)], rd_s.at[0])

        pl.when(z == k)(line)
    trade.wait()
    both = stats[0] + stats[1]
    values = both[:, 1:2] * lax.rsqrt(both[:, 0:1] / (2 * half) + 1e-06)
    members = (marks[...] == lane.astype(f32)).astype(f32)
    sums = jnp.sum(members * values, axis=0, keepdims=True)
    counts = jnp.sum(members, axis=0, keepdims=True)
    rewards[...] = (sums / jnp.maximum(counts, 1.0))[:, :SEQ_GRP]


def routed_layer(tokens, ids, weights, value_row, seq, gate, up, down):
    chunks, rows, half = tokens.shape
    width, units = gate.shape
    bf16 = jnp.bfloat16
    dma = pltpu.SemaphoreType.DMA
    flops = 2 * 16 * GRP * 3 * width * units
    vmem, anywhere = pl.BlockSpec(memory_space=pltpu.VMEM), pl.BlockSpec(memory_space=pl.ANY)
    return pl.pallas_call(
        fused,
        out_shape=(
            jax.ShapeDtypeStruct((GRP, half), bf16),
            jax.ShapeDtypeStruct((1, SEQ_GRP), jnp.float32),
        ),
        in_specs=[anywhere] + [vmem] * 4 + [anywhere] * 3,
        out_specs=(vmem,) * 2,
        scratch_shapes=[
            pltpu.VMEM((2, chunks, 2, 4, 2, rows, half + PAD), bf16),
            pltpu.VMEM((width, units), bf16),
            pltpu.VMEM((width, units), bf16),
            pltpu.VMEM((units, width), bf16),
            pltpu.VMEM((16 * rows, units), bf16),
            pltpu.VMEM((16 * rows, 1), jnp.float32),
            pltpu.VMEM((chunks, 2, 4, 2, rows, half), bf16),
            pltpu.VMEM((chunks, 4, 2, rows, half), bf16),
            pltpu.VMEM((chunks, 3, 2, rows, half), bf16),
            pltpu.VMEM((chunks, 3, 2, rows, half), bf16),
            pltpu.VMEM((chunks, rows, half), bf16),
            pltpu.VMEM((2, GRP, PAD), jnp.float32),
            pltpu.VMEM((GRP, PAD), jnp.float32),
            dma((3,)), dma,
            dma((1,)), dma((chunks,)),
            dma((1,)), dma((chunks, 3)),
            dma((1,)), dma((chunks, 3)),
            dma((1,)), dma((chunks, 4)),
            dma((1,)), dma((chunks,)),
            dma((1,)), dma((chunks,)),
            dma((1,)), dma((chunks, 4)),
            dma((1,)), dma((chunks, 3)),
            dma((1,)), dma((chunks, 3)),
            dma((1,)), dma((chunks,)),
            dma((2,)),
        ],
        compiler_params=pltpu.CompilerParams(
            collective_id=0, has_side_effects=True, vmem_limit_bytes=63 * 1024 * 1024
        ),
        cost_estimate=pl.CostEstimate(
            flops=flops, bytes_accessed=6 * width * units, transcendentals=16 * GRP * units
        ),
    )(tokens, ids, weights, value_row, seq, gate, up, down)


def shards(
    tokens,
    expert_ids,
    route_weights,
    gate_weight,
    up_weight,
    down_weight,
    value_weight,
    sequence_ids,
):
    tok_count, width_part = tokens.shape
    return routed_layer(
        tokens.reshape(tok_count // ROWS, ROWS, width_part), expert_ids, route_weights,
        value_weight[None, :], sequence_ids, gate_weight[0], up_weight[0], down_weight[0],
    )


def solution(mesh):
    in_specs = (
        P("ep", "tp"),
        P("ep", None),
        P("ep", None),
        P("ep", None, "tp"),
        P("ep", None, "tp"),
        P("ep", "tp", None),
        P("tp"),
        P("ep", None),
    )
    out_specs = (P("ep", "tp"), P("ep", None))
    body = shards if dict(mesh.shape) == {"tp": 2, "ep": 16} else plain_shards
    return jax.shard_map(body, mesh=mesh, in_specs=in_specs, out_specs=out_specs, check_vma=False)
```

```python
import functools

import jax
import jax.numpy as jnp
from jax import lax
from jax.experimental import pallas as pl
from jax.experimental.pallas import tpu as pltpu
from jax.sharding import PartitionSpec as P

SEQ_GRP = 4
CHUNKS = 1


def head(layer_output, value_weight, sequence_ids, parts):
    width_part = layer_output.shape[1]
    as_float = layer_output.astype(jnp.float32)
    squares = jnp.sum(as_float * as_float, axis=1)
    along = jnp.sum(as_float * value_weight[None, :], axis=1)
    squares, along = lax.psum((squares, along), "tp")
    values = along * lax.rsqrt(squares / (width_part * parts) + 1e-06)
    members = (sequence_ids[0][None, :] == jnp.arange(SEQ_GRP, dtype=jnp.int32)[:, None]).astype(
        jnp.float32
    )
    sums = jnp.sum(members * values[None, :], axis=1)
    counts = jnp.sum(members, axis=1)
    rewards = sums / counts
    return rewards[None, :]


def plain_shards(
    tokens,
    expert_ids,
    route_weights,
    gate_weight,
    up_weight,
    down_weight,
    value_weight,
    sequence_ids,
):
    tok_count, width_part = tokens.shape
    groups = lax.axis_size("ep")
    parts = lax.axis_size("tp")
    share = route_weights / jnp.sum(route_weights, axis=1, keepdims=True)
    named = expert_ids[:, :, None] == jnp.arange(groups, dtype=jnp.int32)[None, None, :]
    dense = jnp.sum(jnp.where(named, share[:, :, None], 0.0), axis=1)
    dense_all = lax.all_gather(dense, "ep", axis=0)
    mine = lax.dynamic_index_in_dim(dense_all, lax.axis_index("ep"), 2, keepdims=False)
    gate_local = gate_weight[0].reshape(parts, width_part, -1)
    up_local = up_weight[0].reshape(parts, width_part, -1)
    rows = tok_count // CHUNKS
    pieces = []
    for c in range(CHUNKS):
        own = tokens[c * rows:(c + 1) * rows]
        half = lax.all_gather(own, "ep", axis=0, tiled=True)
        full = lax.all_gather(half, "tp", axis=0)
        gate = jnp.einsum("qtd,qdf->tf", full, gate_local, preferred_element_type=jnp.float32)
        upper = jnp.einsum("qtd,qdf->tf", full, up_local, preferred_element_type=jnp.float32)
        scale = mine[:, c * rows:(c + 1) * rows].reshape(groups * rows, 1)
        hidden = (jax.nn.silu(gate) * upper).astype(jnp.bfloat16)
        terms = jnp.dot(hidden, down_weight[0], preferred_element_type=jnp.float32)
        terms = (terms * scale).astype(jnp.bfloat16)
        summed = lax.psum_scatter(terms, "tp", scatter_dimension=1, tiled=True)
        pieces.append(lax.psum_scatter(summed, "ep", scatter_dimension=0, tiled=True))
    routed = jnp.concatenate(pieces, axis=0).astype(jnp.float32)
    layer_output = (tokens.astype(jnp.float32) + routed).astype(jnp.bfloat16)
    return (layer_output, head(layer_output, value_weight, sequence_ids, parts))


MESH = pl.DeviceIdType.MESH
GRP = 128
PAD = 128
EXTRA = 256
ROWS = 16
PLAN = (
    ("fgo", -8.38), ("own", -1.23), ("hop1", -0.35), ("hop2", 0.51), ("hop3", 1.14),
    ("hop4", 1.30), ("sar", 1.91), ("hid", 2.68), ("oth", 2.89), ("mine", 3.58),
    ("ra", 4.94), ("fa", 5.16), ("cs0", 5.27), ("cs1", 6.15), ("cs2", 7.02),
    ("end", 7.95), ("fin", 9.49),
)
AG = "ACCCCCCC"
RS = "CCCCCCCA"
LAST = tuple(c for c, kind in enumerate(RS) if kind == "A")
ORDER = (3, 0, 2, 1)


def runs(labels):
    cuts = [c for c in range(1, len(labels)) if labels[c] != labels[c - 1]]
    return list(zip([0] + cuts, cuts + [len(labels)]))


def run_of(labels, c):
    return sum(labels[i] != labels[i - 1] for i in range(1, c + 1))


def fused(
    tok_hbm, ids, weights, value_row, seq, gate_hbm, up_hbm, down_hbm, out, rewards,
    held, gate_w, up_w, down_w, hid, scale, part, s_in, u_in, d_in, f_in, x_in, stats, marks,
    w_sem, tok_sem, af_s, af_r, au_s, au_r, ad_s, ad_r, as_s, as_r, at_s, at_r,
    sw_s, sw_r, rs_s, rs_r, ru_s, ru_r, rd_s, rd_r, rf_s, rf_r, v_sem,
):
    f32, bf16 = jnp.float32, jnp.bfloat16
    half = out.shape[1]
    chunks = GRP // ROWS
    block = 16 * ROWS
    t = lax.axis_index("tp")
    e = lax.axis_index("ep")
    x = lax.rem(e, 2)
    y = lax.rem(lax.div(e, 2), 2)
    z = lax.div(e, 4)
    e_x = e + 1 - 2 * x
    e_y = e + 2 - 4 * y
    near = (t, e_x * (1 - t) + e_y * t)
    far = (t, e_y * (1 - t) + e_x * t)
    twin = (1 - t, e)
    above = (t, lax.rem(e + 4, 16))
    below = (t, lax.rem(e + 12, 16))
    feats = pl.ds(0, half)

    def remote(src, dst, send, recv, target):
        return pltpu.make_async_remote_copy(
            src_ref=src, dst_ref=dst, send_sem=send, recv_sem=recv,
            device_id=target, device_id_type=MESH,
        )

    def arrived(ref, sem):
        remote(ref, ref, v_sem.at[0], sem, twin).wait_recv()

    def left(ref, sem):
        remote(ref, ref, sem, v_sem.at[1], twin).wait_send()

    load_tok = pltpu.make_async_copy(tok_hbm, held.at[t, :, 0, z, 0, :, feats], tok_sem)
    load_tok.start()
    barrier = pltpu.get_barrier_semaphore()
    for target in (above, below, near, far, twin):
        pl.semaphore_signal(barrier, inc=1, device_id=target, device_id_type=MESH)
    loads = [
        pltpu.make_async_copy(a, b, w_sem.at[i])
        for i, (a, b) in enumerate(((gate_hbm, gate_w), (up_hbm, up_w), (down_hbm, down_w)))
    ]
    for load in loads:
        load.start()

    share = weights[...] / jnp.sum(weights[...], axis=0, keepdims=True)
    row = lax.broadcasted_iota(jnp.int32, (PAD, GRP), 0)
    dense = jnp.zeros((PAD, GRP), f32)
    for k in range(ids.shape[0]):
        dense += jnp.where(lax.rem(row, 16) == ids[k:k + 1], share[k:k + 1], 0.0)
    dense = jnp.transpose(dense)
    lanes = lax.broadcasted_iota(jnp.int32, (ROWS, PAD), 1)
    tile = jnp.zeros((ROWS, PAD), f32)
    for c in range(chunks):
        tile += jnp.where(lax.div(lanes, 16) == c, dense[c * ROWS:(c + 1) * ROWS], 0.0)
    top = tile.astype(bf16)
    held[t, 0, 0, z, 0, :, pl.ds(half, PAD)] = top
    held[t, 0, 0, z, 0, :, pl.ds(half + PAD, PAD)] = (tile - top.astype(f32)).astype(bf16)
    marks[...] = jnp.transpose(jnp.broadcast_to(seq[...].astype(f32), (GRP, PAD)))
    load_tok.wait()
    pl.semaphore_wait(barrier, 5)

    ag_runs = runs([(kind, c == 0) for c, kind in enumerate(AG)])
    rs_runs = runs(RS)

    def ga(c):
        return run_of([(kind, i == 0) for i, kind in enumerate(AG)], c)

    def gr(c):
        return run_of(RS, c)

    def wide(c):
        return pl.ds(0, half + EXTRA) if c == 0 else feats

    def group(c, d, f):
        return held.at[t, c, 0, d, f, :, wide(c)]

    def pair(c, d):
        if AG[c] == "A":
            return group(c, d, 0)
        return held.at[t, c, 0, d, :, :, wide(c)]

    def near_go(c, d):
        remote(group(c, d, 0), group(c, d, 1), af_s.at[ga(c)], af_r.at[c, d], near).start()

    def fgo(c):
        near_go(c, z)

    def up_go(c, k):
        remote(pair(c, z - k), pair(c, z - k), au_s.at[ga(c)], au_r.at[c, k], above).start()

    def down_go(c, k):
        remote(pair(c, z + k), pair(c, z + k), ad_s.at[ga(c)], ad_r.at[c, k], below).start()

    def far_go(c, d):
        if AG[c] == "A":
            arrived(group(c, d, 1), af_r.at[c, d])
        remote(
            held.at[t, c, 0, d, :, :, wide(c)], held.at[t, c, 1, d, :, :, wide(c)],
            as_s.at[ga(c)], as_r.at[c, d], far,
        ).start()

    def twin_go(c, s):
        for f in range(2):
            remote(
                held.at[t, c, s, :, f, :, feats], held.at[t, c, f, :, s, :, feats],
                at_s.at[0], at_r.at[c], twin,
            ).start()

    def own(c):
        if AG[c] == "C":
            arrived(group(c, z, 1), af_r.at[c, z])
        pl.when(z < 3)(lambda: up_go(c, 0))
        pl.when(z > 0)(lambda: down_go(c, 0))
        if AG[c] == "C":
            far_go(c, z)

    def hop(k, c):
        onward = far_go if AG[c] == "C" else near_go

        def from_below():
            arrived(pair(c, z - k), au_r.at[c, k - 1])
            if k < 3:
                pl.when(z < 3)(lambda: up_go(c, k))
            onward(c, z - k)

        def from_above():
            arrived(pair(c, z + k), ad_r.at[c, k - 1])
            if k < 3:
                pl.when(z > 0)(lambda: down_go(c, k))
            onward(c, z + k)

        if k < 4:
            pl.when(z >= k)(from_below)
            pl.when(z + k <= 3)(from_above)
        if AG[c] == "A":
            if k == 1:
                far_go(c, z)
            else:
                pl.when(z >= k - 1)(lambda: far_go(c, z - (k - 1)))
                pl.when(z + k - 1 <= 3)(lambda: far_go(c, z + k - 1))
        if k == (3 if AG[c] == "C" else 4):
            twin_go(c, 0)

    def sar(c):
        for d in range(4):
            arrived(held.at[t, c, 1, d, :, :, wide(c)], as_r.at[c, d])
        twin_go(c, 1)

    def flat(value):
        return value.reshape(block, value.shape[-1])

    def hidden(c):
        if c == 0:
            for load in loads:
                load.wait()
        arrived(held.at[1 - t, c, :, :, :, :, feats], at_r.at[c])
        lanes = lax.broadcasted_iota(jnp.int32, (block, PAD), 1)
        shares = flat(held[t, 0, :, :, :, :, pl.ds(half, PAD)]).astype(f32)
        shares += flat(held[t, 0, :, :, :, :, pl.ds(half + PAD, PAD)]).astype(f32)
        scale[...] = jnp.sum(jnp.where(lanes == c * 16 + e, shares, 0.0), axis=1, keepdims=True)
        a = flat(held[0, c, :, :, :, :, feats])
        b = flat(held[1, c, :, :, :, :, feats])
        g = jnp.dot(a, gate_w[pl.ds(0, half)], preferred_element_type=f32)
        g += jnp.dot(b, gate_w[pl.ds(half, half)], preferred_element_type=f32)
        u = jnp.dot(a, up_w[pl.ds(0, half)], preferred_element_type=f32)
        u += jnp.dot(b, up_w[pl.ds(half, half)], preferred_element_type=f32)
        hid[...] = (g / (1.0 + jnp.exp(-g)) * u * scale[...]).astype(bf16)

    def term(n, core):
        cols = pl.ds(pl.multiple_of(core * half + n * 512, 512), 512)
        return jnp.dot(hid[...], down_w[:, cols], preferred_element_type=f32)

    def other(c):
        def step(n, carry):
            cols = pl.ds(pl.multiple_of(n * 512, 512), 512)
            value = term(n, 1 - t).astype(bf16)
            held[1 - t, c, :, :, :, :, cols] = value.reshape(2, 4, 2, ROWS, 512)
            return carry

        lax.fori_loop(0, half // 512, step, 0)
        for s in range(2):
            for f in range(2):
                remote(
                    held.at[1 - t, c, s, :, f, :, feats], part.at[c, f, :, s],
                    sw_s.at[0], sw_r.at[c], twin,
                ).start()

    def mine(c):
        arrived(part.at[c], sw_r.at[c])

        def step(n, carry):
            cols = pl.ds(pl.multiple_of(n * 512, 512), 512)
            total = term(n, t) + flat(part[c, :, :, :, :, cols]).astype(f32)
            part[c, :, :, :, :, cols] = total.astype(bf16).reshape(2, 4, 2, ROWS, 512)
            return carry

        lax.fori_loop(0, half // 512, step, 0)
        for d in ORDER:
            remote(part.at[c, 1, d], s_in.at[c, d], rs_s.at[0], rs_r.at[c, d], far).start()

    def add(dst, src):
        for f in range(2):
            dst[f] = dst[f] + src[f]

    def add_one(dst, src):
        dst[...] = dst[...] + src[...]

    def ra(c):
        for d in ORDER:
            arrived(s_in.at[c, d], rs_r.at[c, d])
            if RS[c] == "A":
                add_one(part.at[c, 0, d, 1], s_in.at[c, d, 1])
                remote(
                    part.at[c, 0, d, 1], x_in.at[LAST.index(c), d], rf_s.at[gr(c)], rf_r.at[c, d], near
                ).start()
                add_one(part.at[c, 0, d, 0], s_in.at[c, d, 0])
            else:
                add(part.at[c, 0, d], s_in.at[c, d])

    def fa(c):
        if RS[c] == "A":
            for d in ORDER:
                arrived(x_in.at[LAST.index(c), d], rf_r.at[c, d])
                add_one(part.at[c, 0, d, 0], x_in.at[LAST.index(c), d])

    def line_ref(ref, c, d, slot):
        if ref is part:
            return part.at[c, 0, d, 0] if RS[c] == "A" else part.at[c, 0, d]
        return ref.at[c, slot, 0] if RS[c] == "A" else ref.at[c, slot]

    def join(c, d, came, slot, sem):
        arrived(line_ref(came, c, d, slot), sem.at[c, slot])
        plus = add_one if RS[c] == "A" else add
        plus(line_ref(part, c, d, d), line_ref(came, c, d, slot))

    def cs(h, c):
        def up():
            for d in range(3, h, -1):
                if h > 0:
                    join(c, d, u_in, d - 1, ru_r)
                remote(
                    line_ref(part, c, d, d), line_ref(u_in, c, d, d - 1),
                    ru_s.at[gr(c)], ru_r.at[c, d - 1], above,
                ).start()

        def down():
            for d in range(3 - h):
                if h > 0:
                    join(c, d, d_in, d, rd_r)
                remote(
                    line_ref(part, c, d, d), line_ref(d_in, c, d, d),
                    rd_s.at[gr(c)], rd_r.at[c, d], below,
                ).start()

        pl.when(z == h)(up)
        pl.when(z == 3 - h)(down)

    def end(c):
        pl.when(z > 0)(lambda: join(c, z, u_in, z - 1, ru_r))
        pl.when(z < 3)(lambda: join(c, z, d_in, z, rd_r))
        if RS[c] == "C":
            remote(part.at[c, 0, z, 1], f_in.at[c], rf_s.at[gr(c)], rf_r.at[c, z], near).start()

    def fin(c):
        total = part[c, 0, z, 0].astype(f32)
        if RS[c] == "C":
            arrived(f_in.at[c], rf_r.at[c, z])
            total += f_in[c].astype(f32)
        total += held[t, c, 0, z, 0, :, feats].astype(f32)
        rounded = total.astype(bf16)
        rows = pl.ds(c * ROWS, ROWS)
        out[rows] = rounded
        as_float = rounded.astype(f32)
        squares = jnp.sum(as_float * as_float, axis=1, keepdims=True)
        along = jnp.sum(as_float * value_row[...], axis=1, keepdims=True)
        lanes = lax.broadcasted_iota(jnp.int32, (ROWS, PAD), 1)
        stats[0, rows] = jnp.where(lanes == 0, squares, along)

    steps = {
        "fgo": fgo, "own": own, "sar": sar, "hid": hidden, "oth": other, "mine": mine, "ra": ra,
        "fa": fa, "end": end, "fin": fin,
    }
    for k in range(1, 5):
        steps["hop%d" % k] = functools.partial(hop, k)
        steps["cs%d" % (k - 1)] = functools.partial(cs, k - 1)
    turns = [(c + start, i, c, name) for c in range(chunks) for i, (name, start) in enumerate(PLAN)]
    for _, _, c, name in sorted(turns):
        steps[name](c)

    trade = remote(stats.at[0], stats.at[1], v_sem.at[0], v_sem.at[1], twin)
    trade.start()
    left(held.at[t, :, :, :, :, :, feats], at_s.at[0])
    left(part, sw_s.at[0])
    left(part.at[:, 1], rs_s.at[0])
    for i, (first, stop) in enumerate(ag_runs):
        run, w = pl.ds(first, stop - first), wide(first)
        single = AG[first] == "A"
        left(held.at[t, run, 0, pl.ds(0, 4 if single else 1), 0, :, w], af_s.at[i])
        left(held.at[t, run, 0, :, :, :, w], as_s.at[i])
    for i, (first, stop) in enumerate(rs_runs):
        run = pl.ds(first, stop - first)
        left(part.at[run, 0, pl.ds(0, 4 if RS[first] == "A" else 1), 0], rf_s.at[i])

    def line_sent(k):
        for i, (first, stop) in enumerate(ag_runs):
            run, w = pl.ds(first, stop - first), wide(first)
            f = pl.ds(0, 1 if AG[first] == "A" else 2)
            if k < 3:
                left(held.at[t, run, 0, pl.ds(0, k + 1), f, :, w], au_s.at[i])
            if k > 0:
                left(held.at[t, run, 0, pl.ds(0, 4 - k), f, :, w], ad_s.at[i])
        for i, (first, stop) in enumerate(rs_runs):
            run = pl.ds(first, stop - first)
            f = pl.ds(0, 1 if RS[first] == "A" else 2)
            if k < 3:
                left(part.at[run, 0, pl.ds(0, 3 - k), f], ru_s.at[i])
            if k > 0:
                left(part.at[run, 0, pl.ds(0, k), f], rd_s.at[i])

    for k in range(4):
        pl.when(z == k)(functools.partial(line_sent, k))
    trade.wait()
    both = stats[0] + stats[1]
    values = both[:, 1:2] * lax.rsqrt(both[:, 0:1] / (2 * half) + 1e-06)
    lane = lax.broadcasted_iota(jnp.int32, (GRP, PAD), 1)
    members = (marks[...] == lane.astype(f32)).astype(f32)
    sums = jnp.sum(members * values, axis=0, keepdims=True)
    counts = jnp.sum(members, axis=0, keepdims=True)
    rewards[...] = (sums / jnp.maximum(counts, 1.0))[:, :SEQ_GRP]


def routed_layer(tokens, ids, weights, value_row, seq, gate, up, down):
    chunks, rows, half = tokens.shape
    width, units = gate.shape
    bf16 = jnp.bfloat16
    dma = pltpu.SemaphoreType.DMA
    flops = 2 * 16 * GRP * 3 * width * units
    vmem, anywhere = pl.BlockSpec(memory_space=pltpu.VMEM), pl.BlockSpec(memory_space=pl.ANY)
    return pl.pallas_call(
        fused,
        out_shape=(
            jax.ShapeDtypeStruct((GRP, half), bf16),
            jax.ShapeDtypeStruct((1, SEQ_GRP), jnp.float32),
        ),
        in_specs=[anywhere] + [vmem] * 4 + [anywhere] * 3,
        out_specs=(vmem,) * 2,
        scratch_shapes=[
            pltpu.VMEM((2, chunks, 2, 4, 2, rows, half + EXTRA), bf16),
            pltpu.VMEM((width, units), bf16),
            pltpu.VMEM((width, units), bf16),
            pltpu.VMEM((units, width), bf16),
            pltpu.VMEM((16 * rows, units), bf16),
            pltpu.VMEM((16 * rows, 1), jnp.float32),
            pltpu.VMEM((chunks, 2, 4, 2, rows, half), bf16),
            pltpu.VMEM((chunks, 4, 2, rows, half), bf16),
            pltpu.VMEM((chunks, 3, 2, rows, half), bf16),
            pltpu.VMEM((chunks, 3, 2, rows, half), bf16),
            pltpu.VMEM((chunks, rows, half), bf16),
            pltpu.VMEM((max(1, len(LAST)), 4, rows, half), bf16),
            pltpu.VMEM((2, GRP, PAD), jnp.float32),
            pltpu.VMEM((GRP, PAD), jnp.float32),
            dma((3,)), dma,
            dma((chunks,)), dma((chunks, 4)),
            dma((chunks,)), dma((chunks, 3)),
            dma((chunks,)), dma((chunks, 3)),
            dma((chunks,)), dma((chunks, 4)),
            dma((1,)), dma((chunks,)),
            dma((1,)), dma((chunks,)),
            dma((1,)), dma((chunks, 4)),
            dma((chunks,)), dma((chunks, 3)),
            dma((chunks,)), dma((chunks, 3)),
            dma((chunks,)), dma((chunks, 4)),
            dma((2,)),
        ],
        compiler_params=pltpu.CompilerParams(
            collective_id=0, has_side_effects=True, vmem_limit_bytes=63 * 1024 * 1024
        ),
        cost_estimate=pl.CostEstimate(
            flops=flops, bytes_accessed=6 * width * units, transcendentals=16 * GRP * units
        ),
    )(tokens, ids, weights, value_row, seq, gate, up, down)


def shards(
    tokens,
    expert_ids,
    route_weights,
    gate_weight,
    up_weight,
    down_weight,
    value_weight,
    sequence_ids,
):
    tok_count, width_part = tokens.shape
    return routed_layer(
        tokens.reshape(tok_count // ROWS, ROWS, width_part), expert_ids.T, route_weights.T,
        value_weight[None, :], sequence_ids, gate_weight[0], up_weight[0], down_weight[0],
    )


def solution(mesh):
    in_specs = (
        P("ep", "tp"),
        P("ep", None),
        P("ep", None),
        P("ep", None, "tp"),
        P("ep", None, "tp"),
        P("ep", "tp", None),
        P("tp"),
        P("ep", None),
    )
    out_specs = (P("ep", "tp"), P("ep", None))
    body = shards if dict(mesh.shape) == {"tp": 2, "ep": 16} else plain_shards
    return jax.shard_map(body, mesh=mesh, in_specs=in_specs, out_specs=out_specs, check_vma=False)
```

```python
import functools

import jax
import jax.numpy as jnp
from jax import lax
from jax.experimental import pallas as pl
from jax.experimental.pallas import tpu as pltpu
from jax.sharding import PartitionSpec as P

SEQ_GRP = 4
CHUNKS = 1


def head(layer_output, value_weight, sequence_ids, parts):
    width_part = layer_output.shape[1]
    as_float = layer_output.astype(jnp.float32)
    squares = jnp.sum(as_float * as_float, axis=1)
    along = jnp.sum(as_float * value_weight[None, :], axis=1)
    squares, along = lax.psum((squares, along), "tp")
    values = along * lax.rsqrt(squares / (width_part * parts) + 1e-06)
    members = (sequence_ids[0][None, :] == jnp.arange(SEQ_GRP, dtype=jnp.int32)[:, None]).astype(
        jnp.float32
    )
    sums = jnp.sum(members * values[None, :], axis=1)
    counts = jnp.sum(members, axis=1)
    rewards = sums / counts
    return rewards[None, :]


def plain_shards(
    tokens,
    expert_ids,
    route_weights,
    gate_weight,
    up_weight,
    down_weight,
    value_weight,
    sequence_ids,
):
    tok_count, width_part = tokens.shape
    groups = lax.axis_size("ep")
    parts = lax.axis_size("tp")
    share = route_weights / jnp.sum(route_weights, axis=1, keepdims=True)
    named = expert_ids[:, :, None] == jnp.arange(groups, dtype=jnp.int32)[None, None, :]
    dense = jnp.sum(jnp.where(named, share[:, :, None], 0.0), axis=1)
    dense_all = lax.all_gather(dense, "ep", axis=0)
    mine = lax.dynamic_index_in_dim(dense_all, lax.axis_index("ep"), 2, keepdims=False)
    gate_local = gate_weight[0].reshape(parts, width_part, -1)
    up_local = up_weight[0].reshape(parts, width_part, -1)
    rows = tok_count // CHUNKS
    pieces = []
    for c in range(CHUNKS):
        own = tokens[c * rows:(c + 1) * rows]
        half = lax.all_gather(own, "ep", axis=0, tiled=True)
        full = lax.all_gather(half, "tp", axis=0)
        gate = jnp.einsum("qtd,qdf->tf", full, gate_local, preferred_element_type=jnp.float32)
        upper = jnp.einsum("qtd,qdf->tf", full, up_local, preferred_element_type=jnp.float32)
        scale = mine[:, c * rows:(c + 1) * rows].reshape(groups * rows, 1)
        hidden = (jax.nn.silu(gate) * upper).astype(jnp.bfloat16)
        terms = jnp.dot(hidden, down_weight[0], preferred_element_type=jnp.float32)
        terms = (terms * scale).astype(jnp.bfloat16)
        summed = lax.psum_scatter(terms, "tp", scatter_dimension=1, tiled=True)
        pieces.append(lax.psum_scatter(summed, "ep", scatter_dimension=0, tiled=True))
    routed = jnp.concatenate(pieces, axis=0).astype(jnp.float32)
    layer_output = (tokens.astype(jnp.float32) + routed).astype(jnp.bfloat16)
    return (layer_output, head(layer_output, value_weight, sequence_ids, parts))


MESH = pl.DeviceIdType.MESH
GRP = 128
PAD = 128
EXTRA = 256
ROWS = 16
PLAN = (
    ("fgo", -2.30), ("own", -1.23), ("hop1", -0.35), ("hop2", 0.51), ("hop3", 1.14),
    ("hop4", 1.30), ("sar", 1.91), ("hid", 2.68), ("oth", 2.89), ("mine", 3.58),
    ("ra", 5.14), ("fa", 5.36), ("cs0", 5.47), ("cs1", 6.35), ("cs2", 7.22),
    ("end", 8.15), ("fin", 9.69), ("e2", 8.70),
)
AG = "AACCCCCC"
RS = "CCCCCCCA"
LAST = tuple(c for c, kind in enumerate(RS) if kind == "A")
QUADS = tuple(c for c, kind in enumerate(RS) if kind == "B")
ORDER = (3, 0, 2, 1)


def runs(labels):
    cuts = [c for c in range(1, len(labels)) if labels[c] != labels[c - 1]]
    return list(zip([0] + cuts, cuts + [len(labels)]))


def run_of(labels, c):
    return sum(labels[i] != labels[i - 1] for i in range(1, c + 1))


def fused(
    tok_hbm, ids, weights, value_row, seq, gate_hbm, up_hbm, down_hbm, out, rewards,
    held, gate_w, up_w, down_w, hid, scale, own_part, part, s_in, u_in, d_in, f_in, x_in, q_in, stats, marks,
    w_sem, tok_sem, af_s, af_r, au_s, au_r, ad_s, ad_r, as_s, as_r, at_s, at_r,
    sw_s, sw_r, rs_s, rs_r, ru_s, ru_r, rd_s, rd_r, rf_s, rf_r, v_sem,
):
    f32, bf16 = jnp.float32, jnp.bfloat16
    half = out.shape[1]
    chunks = GRP // ROWS
    block = 16 * ROWS
    t = lax.axis_index("tp")
    e = lax.axis_index("ep")
    x = lax.rem(e, 2)
    y = lax.rem(lax.div(e, 2), 2)
    z = lax.div(e, 4)
    e_x = e + 1 - 2 * x
    e_y = e + 2 - 4 * y
    near = (t, e_x * (1 - t) + e_y * t)
    far = (t, e_y * (1 - t) + e_x * t)
    twin = (1 - t, e)
    above = (t, lax.rem(e + 4, 16))
    below = (t, lax.rem(e + 12, 16))
    feats = pl.ds(0, half)

    def remote(src, dst, send, recv, target):
        return pltpu.make_async_remote_copy(
            src_ref=src, dst_ref=dst, send_sem=send, recv_sem=recv,
            device_id=target, device_id_type=MESH,
        )

    def arrived(ref, sem):
        remote(ref, ref, v_sem.at[0], sem, twin).wait_recv()

    def left(ref, sem):
        remote(ref, ref, sem, v_sem.at[1], twin).wait_send()

    load_tok = pltpu.make_async_copy(tok_hbm, held.at[t, :, 0, z, 0, :, feats], tok_sem)
    load_tok.start()
    barrier = pltpu.get_barrier_semaphore()
    for target in (above, below, near, far, twin):
        pl.semaphore_signal(barrier, inc=1, device_id=target, device_id_type=MESH)
    loads = [
        pltpu.make_async_copy(a, b, w_sem.at[i])
        for i, (a, b) in enumerate(((gate_hbm, gate_w), (up_hbm, up_w), (down_hbm, down_w)))
    ]
    for load in loads:
        load.start()

    share = weights[...] / jnp.sum(weights[...], axis=0, keepdims=True)
    row = lax.broadcasted_iota(jnp.int32, (PAD, GRP), 0)
    dense = jnp.zeros((PAD, GRP), f32)
    for k in range(ids.shape[0]):
        dense += jnp.where(lax.rem(row, 16) == ids[k:k + 1], share[k:k + 1], 0.0)
    dense = jnp.transpose(dense)
    lanes = lax.broadcasted_iota(jnp.int32, (ROWS, PAD), 1)
    tile = jnp.zeros((ROWS, PAD), f32)
    for c in range(chunks):
        tile += jnp.where(lax.div(lanes, 16) == c, dense[c * ROWS:(c + 1) * ROWS], 0.0)
    top = tile.astype(bf16)
    held[t, 0, 0, z, 0, :, pl.ds(half, PAD)] = top
    held[t, 0, 0, z, 0, :, pl.ds(half + PAD, PAD)] = (tile - top.astype(f32)).astype(bf16)
    marks[...] = jnp.transpose(jnp.broadcast_to(seq[...].astype(f32), (GRP, PAD)))
    load_tok.wait()
    pl.semaphore_wait(barrier, 5)

    ag_runs = runs([(kind, c == 0) for c, kind in enumerate(AG)])
    rs_runs = runs(RS)

    def ga(c):
        return run_of([(kind, i == 0) for i, kind in enumerate(AG)], c)

    def gr(c):
        return run_of(RS, c)

    def wide(c):
        return pl.ds(0, half + EXTRA) if c == 0 else feats

    def group(c, d, f):
        return held.at[t, c, 0, d, f, :, wide(c)]

    def pair(c, d):
        if AG[c] == "A":
            return group(c, d, 0)
        if AG[c] == "B":
            return held.at[t, c, :, d, :, :, wide(c)]
        return held.at[t, c, 0, d, :, :, wide(c)]

    def near_go(c, d):
        remote(group(c, d, 0), group(c, d, 1), af_s.at[ga(c)], af_r.at[c, d], near).start()

    def fgo(c):
        near_go(c, z)

    def up_go(c, k):
        remote(pair(c, z - k), pair(c, z - k), au_s.at[ga(c)], au_r.at[c, k], above).start()

    def down_go(c, k):
        remote(pair(c, z + k), pair(c, z + k), ad_s.at[ga(c)], ad_r.at[c, k], below).start()

    def far_go(c, d):
        if AG[c] == "A":
            arrived(group(c, d, 1), af_r.at[c, d])
        remote(
            held.at[t, c, 0, d, :, :, wide(c)], held.at[t, c, 1, d, :, :, wide(c)],
            as_s.at[ga(c)], as_r.at[c, d], far,
        ).start()

    def twin_go(c, s):
        for f in range(2):
            remote(
                held.at[t, c, s, :, f, :, feats], held.at[t, c, f, :, s, :, feats],
                at_s.at[0], at_r.at[c], twin,
            ).start()

    def line_go(c):
        pl.when(z < 3)(lambda: up_go(c, 0))
        pl.when(z > 0)(lambda: down_go(c, 0))

    def own(c):
        if AG[c] != "A":
            arrived(group(c, z, 1), af_r.at[c, z])
        if AG[c] != "B":
            line_go(c)
        if AG[c] != "A":
            far_go(c, z)

    def hop(k, c):
        onward = {"A": near_go, "B": None, "C": far_go}[AG[c]]
        last = k == (3 if AG[c] == "C" else 4)
        if AG[c] == "B":
            k -= 1

        def from_below():
            arrived(pair(c, z - k), au_r.at[c, k - 1])
            if k < 3:
                pl.when(z < 3)(lambda: up_go(c, k))
            if onward:
                onward(c, z - k)

        def from_above():
            arrived(pair(c, z + k), ad_r.at[c, k - 1])
            if k < 3:
                pl.when(z > 0)(lambda: down_go(c, k))
            if onward:
                onward(c, z + k)

        if k == 0:
            arrived(held.at[t, c, 1, z, :, :, wide(c)], as_r.at[c, z])
            line_go(c)
        elif k < 4:
            pl.when(z >= k)(from_below)
            pl.when(z + k <= 3)(from_above)
        if AG[c] == "A":
            if k == 1:
                far_go(c, z)
            else:
                pl.when(z >= k - 1)(lambda: far_go(c, z - (k - 1)))
                pl.when(z + k - 1 <= 3)(lambda: far_go(c, z + k - 1))
        if last:
            twin_go(c, 0)
            if AG[c] == "B":
                twin_go(c, 1)

    def sar(c):
        if AG[c] == "B":
            return
        for d in range(4):
            arrived(held.at[t, c, 1, d, :, :, wide(c)], as_r.at[c, d])
        twin_go(c, 1)

    def flat(value):
        return value.reshape(block, value.shape[-1])

    def hidden(c):
        if c == 0:
            for load in loads:
                load.wait()
        arrived(held.at[1 - t, c, :, :, :, :, feats], at_r.at[c])
        lanes = lax.broadcasted_iota(jnp.int32, (block, PAD), 1)
        shares = flat(held[t, 0, :, :, :, :, pl.ds(half, PAD)]).astype(f32)
        shares += flat(held[t, 0, :, :, :, :, pl.ds(half + PAD, PAD)]).astype(f32)
        scale[...] = jnp.sum(jnp.where(lanes == c * 16 + e, shares, 0.0), axis=1, keepdims=True)
        a = flat(held[0, c, :, :, :, :, feats])
        b = flat(held[1, c, :, :, :, :, feats])
        g = jnp.dot(a, gate_w[pl.ds(0, half)], preferred_element_type=f32)
        g += jnp.dot(b, gate_w[pl.ds(half, half)], preferred_element_type=f32)
        u = jnp.dot(a, up_w[pl.ds(0, half)], preferred_element_type=f32)
        u += jnp.dot(b, up_w[pl.ds(half, half)], preferred_element_type=f32)
        hid[...] = (g / (1.0 + jnp.exp(-g)) * u * scale[...]).astype(bf16)

    def term(n, core):
        cols = pl.ds(pl.multiple_of(core * half + n * 512, 512), 512)
        return jnp.dot(hid[...], down_w[:, cols], preferred_element_type=f32)

    def other(c):
        def step(n, carry):
            cols = pl.ds(pl.multiple_of(n * 512, 512), 512)
            value = term(n, 1 - t).astype(bf16)
            held[1 - t, c, :, :, :, :, cols] = value.reshape(2, 4, 2, ROWS, 512)
            return carry

        lax.fori_loop(0, half // 512, step, 0)
        for s in range(2):
            for f in range(2):
                remote(
                    held.at[1 - t, c, s, :, f, :, feats], part.at[c, f, :, s],
                    sw_s.at[0], sw_r.at[c], twin,
                ).start()

    def mine(c):
        def step(n, carry):
            cols = pl.ds(pl.multiple_of(n * 512, 512), 512)
            value = term(n, t).astype(bf16)
            own_part[:, :, :, :, cols] = value.reshape(2, 4, 2, ROWS, 512)
            return carry

        lax.fori_loop(0, half // 512, step, 0)
        arrived(part.at[c], sw_r.at[c])
        for d in ORDER:
            add(part.at[c, 1, d], own_part.at[1, d])
            if RS[c] != "B":
                cross(c, d)
        for d in ORDER:
            add(part.at[c, 0, d], own_part.at[0, d])

    def cross(c, d):
        remote(part.at[c, 1, d], s_in.at[c, d], rs_s.at[gr(c)], rs_r.at[c, d], far).start()

    def add(dst, src):
        if len(dst.shape) > 2:
            for f in range(2):
                add(dst.at[f], src.at[f])
        else:
            dst[...] = dst[...] + src[...]

    def ra(c):
        if RS[c] == "B":
            return
        for d in ORDER:
            arrived(s_in.at[c, d], rs_r.at[c, d])
            if RS[c] == "A":
                add(part.at[c, 0, d, 1], s_in.at[c, d, 1])
                remote(
                    part.at[c, 0, d, 1], x_in.at[LAST.index(c), d], rf_s.at[gr(c)], rf_r.at[c, d], near
                ).start()
                add(part.at[c, 0, d, 0], s_in.at[c, d, 0])
            else:
                add(part.at[c, 0, d], s_in.at[c, d])

    def fa(c):
        if RS[c] == "A":
            for d in ORDER:
                arrived(x_in.at[LAST.index(c), d], rf_r.at[c, d])
                add(part.at[c, 0, d, 0], x_in.at[LAST.index(c), d])

    def line_ref(c, d):
        if RS[c] == "B":
            return part.at[c, :, d]
        return part.at[c, 0, d, 0] if RS[c] == "A" else part.at[c, 0, d]

    def came_ref(way, c, slot):
        if RS[c] == "B":
            return q_in.at[way, QUADS.index(c), slot]
        ref = (u_in, d_in)[way]
        return ref.at[c, slot, 0] if RS[c] == "A" else ref.at[c, slot]

    def join(way, c, d, slot):
        arrived(came_ref(way, c, slot), (ru_r, rd_r)[way].at[c, slot])
        add(line_ref(c, d), came_ref(way, c, slot))

    def cs(h, c):
        def up():
            for d in range(3, h, -1):
                if h > 0:
                    join(0, c, d, d - 1)
                remote(
                    line_ref(c, d), came_ref(0, c, d - 1),
                    ru_s.at[gr(c)], ru_r.at[c, d - 1], above,
                ).start()

        def down():
            for d in range(3 - h):
                if h > 0:
                    join(1, c, d, d)
                remote(
                    line_ref(c, d), came_ref(1, c, d),
                    rd_s.at[gr(c)], rd_r.at[c, d], below,
                ).start()

        pl.when(z == h)(up)
        pl.when(z == 3 - h)(down)

    def end(c):
        pl.when(z > 0)(lambda: join(0, c, z, z - 1))
        pl.when(z < 3)(lambda: join(1, c, z, z))
        if RS[c] == "C":
            hand(c)
        if RS[c] == "B":
            cross(c, z)

    def hand(c):
        remote(part.at[c, 0, z, 1], f_in.at[c], rf_s.at[gr(c)], rf_r.at[c, z], near).start()

    def e2(c):
        if RS[c] == "B":
            arrived(s_in.at[c, z], rs_r.at[c, z])
            add(part.at[c, 0, z, 1], s_in.at[c, z, 1])
            hand(c)
            add(part.at[c, 0, z, 0], s_in.at[c, z, 0])

    def fin(c):
        total = part[c, 0, z, 0].astype(f32)
        if RS[c] != "A":
            arrived(f_in.at[c], rf_r.at[c, z])
            total += f_in[c].astype(f32)
        total += held[t, c, 0, z, 0, :, feats].astype(f32)
        rounded = total.astype(bf16)
        rows = pl.ds(c * ROWS, ROWS)
        out[rows] = rounded
        as_float = rounded.astype(f32)
        squares = jnp.sum(as_float * as_float, axis=1, keepdims=True)
        along = jnp.sum(as_float * value_row[...], axis=1, keepdims=True)
        lanes = lax.broadcasted_iota(jnp.int32, (ROWS, PAD), 1)
        stats[0, rows] = jnp.where(lanes == 0, squares, along)

    steps = {
        "fgo": fgo, "own": own, "sar": sar, "hid": hidden, "oth": other, "mine": mine, "ra": ra,
        "fa": fa, "end": end, "e2": e2, "fin": fin,
    }
    for k in range(1, 5):
        steps["hop%d" % k] = functools.partial(hop, k)
        steps["cs%d" % (k - 1)] = functools.partial(cs, k - 1)
    turns = [(c + start, i, c, name) for c in range(chunks) for i, (name, start) in enumerate(PLAN)]
    for _, _, c, name in sorted(turns):
        steps[name](c)

    trade = remote(stats.at[0], stats.at[1], v_sem.at[0], v_sem.at[1], twin)
    trade.start()
    left(held.at[t, :, :, :, :, :, feats], at_s.at[0])
    left(part, sw_s.at[0])
    for i, (first, stop) in enumerate(ag_runs):
        run, w = pl.ds(first, stop - first), wide(first)
        single = AG[first] == "A"
        left(held.at[t, run, 0, pl.ds(0, 4 if single else 1), 0, :, w], af_s.at[i])
        left(held.at[t, run, 0, pl.ds(0, 1 if AG[first] == "B" else 4), :, :, w], as_s.at[i])
    for i, (first, stop) in enumerate(rs_runs):
        run = pl.ds(first, stop - first)
        left(part.at[run, 0, pl.ds(0, 4 if RS[first] == "A" else 1), 0], rf_s.at[i])
        left(part.at[run, 1, pl.ds(0, 1 if RS[first] == "B" else 4)], rs_s.at[i])

    def line_sent(k):
        for i, (first, stop) in enumerate(ag_runs):
            run, w = pl.ds(first, stop - first), wide(first)
            f = pl.ds(0, 1 if AG[first] == "A" else 2)
            r = pl.ds(0, 2 if AG[first] == "B" else 1)
            if k < 3:
                left(held.at[t, run, r, pl.ds(0, k + 1), f, :, w], au_s.at[i])
            if k > 0:
                left(held.at[t, run, r, pl.ds(0, 4 - k), f, :, w], ad_s.at[i])
        for i, (first, stop) in enumerate(rs_runs):
            run = pl.ds(first, stop - first)
            f = pl.ds(0, 1 if RS[first] == "A" else 2)
            r = pl.ds(0, 2 if RS[first] == "B" else 1)
            if k < 3:
                left(part.at[run, r, pl.ds(0, 3 - k), f], ru_s.at[i])
            if k > 0:
                left(part.at[run, r, pl.ds(0, k), f], rd_s.at[i])

    for k in range(4):
        pl.when(z == k)(functools.partial(line_sent, k))
    trade.wait()
    both = stats[0] + stats[1]
    values = both[:, 1:2] * lax.rsqrt(both[:, 0:1] / (2 * half) + 1e-06)
    lane = lax.broadcasted_iota(jnp.int32, (GRP, PAD), 1)
    members = (marks[...] == lane.astype(f32)).astype(f32)
    sums = jnp.sum(members * values, axis=0, keepdims=True)
    counts = jnp.sum(members, axis=0, keepdims=True)
    rewards[...] = (sums / jnp.maximum(counts, 1.0))[:, :SEQ_GRP]


def routed_layer(tokens, ids, weights, value_row, seq, gate, up, down):
    chunks, rows, half = tokens.shape
    width, units = gate.shape
    bf16 = jnp.bfloat16
    dma = pltpu.SemaphoreType.DMA
    flops = 2 * 16 * GRP * 3 * width * units
    vmem, anywhere = pl.BlockSpec(memory_space=pltpu.VMEM), pl.BlockSpec(memory_space=pl.ANY)
    return pl.pallas_call(
        fused,
        out_shape=(
            jax.ShapeDtypeStruct((GRP, half), bf16),
            jax.ShapeDtypeStruct((1, SEQ_GRP), jnp.float32),
        ),
        in_specs=[anywhere] + [vmem] * 4 + [anywhere] * 3,
        out_specs=(vmem,) * 2,
        scratch_shapes=[
            pltpu.VMEM((2, chunks, 2, 4, 2, rows, half + EXTRA), bf16),
            pltpu.VMEM((width, units), bf16),
            pltpu.VMEM((width, units), bf16),
            pltpu.VMEM((units, width), bf16),
            pltpu.VMEM((16 * rows, units), bf16),
            pltpu.VMEM((16 * rows, 1), jnp.float32),
            pltpu.VMEM((2, 4, 2, rows, half), bf16),
            pltpu.VMEM((chunks, 2, 4, 2, rows, half), bf16),
            pltpu.VMEM((chunks, 4, 2, rows, half), bf16),
            pltpu.VMEM((chunks, 3, 2, rows, half), bf16),
            pltpu.VMEM((chunks, 3, 2, rows, half), bf16),
            pltpu.VMEM((chunks, rows, half), bf16),
            pltpu.VMEM((max(1, len(LAST)), 4, rows, half), bf16),
            pltpu.VMEM((2, max(1, len(QUADS)), 3, 2, 2, rows, half if QUADS else PAD), bf16),
            pltpu.VMEM((2, GRP, PAD), jnp.float32),
            pltpu.VMEM((GRP, PAD), jnp.float32),
            dma((3,)), dma,
            dma((chunks,)), dma((chunks, 4)),
            dma((chunks,)), dma((chunks, 3)),
            dma((chunks,)), dma((chunks, 3)),
            dma((chunks,)), dma((chunks, 4)),
            dma((1,)), dma((chunks,)),
            dma((1,)), dma((chunks,)),
            dma((chunks,)), dma((chunks, 4)),
            dma((chunks,)), dma((chunks, 3)),
            dma((chunks,)), dma((chunks, 3)),
            dma((chunks,)), dma((chunks, 4)),
            dma((2,)),
        ],
        compiler_params=pltpu.CompilerParams(
            collective_id=0, has_side_effects=True, vmem_limit_bytes=63 * 1024 * 1024
        ),
        cost_estimate=pl.CostEstimate(
            flops=flops, bytes_accessed=6 * width * units, transcendentals=16 * GRP * units
        ),
    )(tokens, ids, weights, value_row, seq, gate, up, down)


def shards(
    tokens,
    expert_ids,
    route_weights,
    gate_weight,
    up_weight,
    down_weight,
    value_weight,
    sequence_ids,
):
    tok_count, width_part = tokens.shape
    return routed_layer(
        tokens.reshape(tok_count // ROWS, ROWS, width_part), expert_ids.T, route_weights.T,
        value_weight[None, :], sequence_ids, gate_weight[0], up_weight[0], down_weight[0],
    )


def solution(mesh):
    in_specs = (
        P("ep", "tp"),
        P("ep", None),
        P("ep", None),
        P("ep", None, "tp"),
        P("ep", None, "tp"),
        P("ep", "tp", None),
        P("tp"),
        P("ep", None),
    )
    out_specs = (P("ep", "tp"), P("ep", None))
    body = shards if dict(mesh.shape) == {"tp": 2, "ep": 16} else plain_shards
    return jax.shard_map(body, mesh=mesh, in_specs=in_specs, out_specs=out_specs, check_vma=False)
```

```python
import functools

import jax
import jax.numpy as jnp
from jax import lax
from jax.experimental import pallas as pl
from jax.experimental.pallas import tpu as pltpu
from jax.sharding import PartitionSpec as P

SEQ_GRP = 4
CHUNKS = 1


def head(layer_output, value_weight, sequence_ids, parts):
    width_part = layer_output.shape[1]
    as_float = layer_output.astype(jnp.float32)
    squares = jnp.sum(as_float * as_float, axis=1)
    along = jnp.sum(as_float * value_weight[None, :], axis=1)
    squares, along = lax.psum((squares, along), "tp")
    values = along * lax.rsqrt(squares / (width_part * parts) + 1e-06)
    members = (sequence_ids[0][None, :] == jnp.arange(SEQ_GRP, dtype=jnp.int32)[:, None]).astype(
        jnp.float32
    )
    sums = jnp.sum(members * values[None, :], axis=1)
    counts = jnp.sum(members, axis=1)
    rewards = sums / counts
    return rewards[None, :]


def plain_shards(
    tokens,
    expert_ids,
    route_weights,
    gate_weight,
    up_weight,
    down_weight,
    value_weight,
    sequence_ids,
):
    tok_count, width_part = tokens.shape
    groups = lax.axis_size("ep")
    parts = lax.axis_size("tp")
    share = route_weights / jnp.sum(route_weights, axis=1, keepdims=True)
    named = expert_ids[:, :, None] == jnp.arange(groups, dtype=jnp.int32)[None, None, :]
    dense = jnp.sum(jnp.where(named, share[:, :, None], 0.0), axis=1)
    dense_all = lax.all_gather(dense, "ep", axis=0)
    mine = lax.dynamic_index_in_dim(dense_all, lax.axis_index("ep"), 2, keepdims=False)
    gate_local = gate_weight[0].reshape(parts, width_part, -1)
    up_local = up_weight[0].reshape(parts, width_part, -1)
    rows = tok_count // CHUNKS
    pieces = []
    for c in range(CHUNKS):
        own = tokens[c * rows:(c + 1) * rows]
        half = lax.all_gather(own, "ep", axis=0, tiled=True)
        full = lax.all_gather(half, "tp", axis=0)
        gate = jnp.einsum("qtd,qdf->tf", full, gate_local, preferred_element_type=jnp.float32)
        upper = jnp.einsum("qtd,qdf->tf", full, up_local, preferred_element_type=jnp.float32)
        scale = mine[:, c * rows:(c + 1) * rows].reshape(groups * rows, 1)
        hidden = (jax.nn.silu(gate) * upper).astype(jnp.bfloat16)
        terms = jnp.dot(hidden, down_weight[0], preferred_element_type=jnp.float32)
        terms = (terms * scale).astype(jnp.bfloat16)
        summed = lax.psum_scatter(terms, "tp", scatter_dimension=1, tiled=True)
        pieces.append(lax.psum_scatter(summed, "ep", scatter_dimension=0, tiled=True))
    routed = jnp.concatenate(pieces, axis=0).astype(jnp.float32)
    layer_output = (tokens.astype(jnp.float32) + routed).astype(jnp.bfloat16)
    return (layer_output, head(layer_output, value_weight, sequence_ids, parts))


MESH = pl.DeviceIdType.MESH
GRP = 128
PAD = 128
EXTRA = 256
ROWS = 16
PLAN = (
    ("fgo", (2, 0, 1, 3, 4, 6, 8, 9)),
    ("own", (5, 10, 13, 16, 20, 26, 37, 49)),
    ("hop1", (7, 12, 18, 21, 28, 35, 50, 63)),
    ("hop2", (11, 17, 25, 31, 40, 52, 65, 82)),
    ("hop3", (14, 22, 33, 39, 48, 61, 77, 89)),
    ("hop4", (15, 30, 43, 55, 64, 75, 92, 101)),
    ("sar", (19, 27, 41, 47, 60, 73, 84, 98)),
    ("hid", (23, 32, 45, 57, 66, 79, 93, 103)),
    ("oth", (24, 34, 46, 58, 67, 80, 94, 104)),
    ("mine", (29, 38, 56, 62, 74, 83, 99, 108)),
    ("ra", (36, 51, 68, 76, 86, 96, 109, 113)),
    ("fa", (42, 53, 69, 78, 88, 97, 110, 121)),
    ("cs0", (44, 54, 72, 81, 91, 100, 111, 122)),
    ("cs1", (59, 71, 85, 95, 105, 112, 116, 128)),
    ("cs2", (70, 87, 102, 107, 114, 118, 125, 135)),
    ("end", (90, 106, 115, 117, 124, 127, 132, 139)),
    ("e2", (119, 120, 126, 130, 133, 137, 140, 141)),
    ("fin", (134, 123, 129, 131, 136, 138, 142, 143)),
)
AG = "ACCCCCCC"
RS = "BCCCCCCA"
LAST = tuple(c for c, kind in enumerate(RS) if kind == "A")
QUADS = tuple(c for c, kind in enumerate(RS) if kind == "B")
ORDER = (3, 0, 2, 1)


def runs(labels):
    cuts = [c for c in range(1, len(labels)) if labels[c] != labels[c - 1]]
    return list(zip([0] + cuts, cuts + [len(labels)]))


def run_of(labels, c):
    return sum(labels[i] != labels[i - 1] for i in range(1, c + 1))


def fused(
    tok_hbm, ids, weights, value_row, seq, gate_hbm, up_hbm, down_hbm, out, rewards,
    held, gate_w, up_w, down_w, hid, scale, own_part, part, s_in, u_in, d_in, f_in, x_in, q_in, stats, marks, stage,
    w_sem, tok_sem, out_sem, af_s, af_r, au_s, au_r, ad_s, ad_r, as_s, as_r, at_s, at_r,
    sw_s, sw_r, rs_s, rs_r, ru_s, ru_r, rd_s, rd_r, rf_s, rf_r, v_sem,
):
    f32, bf16 = jnp.float32, jnp.bfloat16
    half = out.shape[1]
    chunks = GRP // ROWS
    block = 16 * ROWS
    t = lax.axis_index("tp")
    e = lax.axis_index("ep")
    x = lax.rem(e, 2)
    y = lax.rem(lax.div(e, 2), 2)
    z = lax.div(e, 4)
    e_x = e + 1 - 2 * x
    e_y = e + 2 - 4 * y
    near = (t, e_x * (1 - t) + e_y * t)
    far = (t, e_y * (1 - t) + e_x * t)
    twin = (1 - t, e)
    above = (t, lax.rem(e + 4, 16))
    below = (t, lax.rem(e + 12, 16))
    feats = pl.ds(0, half)

    def remote(src, dst, send, recv, target):
        return pltpu.make_async_remote_copy(
            src_ref=src, dst_ref=dst, send_sem=send, recv_sem=recv,
            device_id=target, device_id_type=MESH,
        )

    def arrived(ref, sem):
        remote(ref, ref, v_sem.at[0], sem, twin).wait_recv()

    def left(ref, sem):
        remote(ref, ref, sem, v_sem.at[1], twin).wait_send()

    load_tok = pltpu.make_async_copy(tok_hbm, held.at[t, :, 0, z, 0, :, feats], tok_sem)
    load_tok.start()
    barrier = pltpu.get_barrier_semaphore()
    for target in (above, below, near, far, twin):
        pl.semaphore_signal(barrier, inc=1, device_id=target, device_id_type=MESH)
    loads = [
        pltpu.make_async_copy(a, b, w_sem.at[i])
        for i, (a, b) in enumerate(((gate_hbm, gate_w), (up_hbm, up_w), (down_hbm, down_w)))
    ]
    for load in loads:
        load.start()

    share = weights[...] / jnp.sum(weights[...], axis=0, keepdims=True)
    row = lax.broadcasted_iota(jnp.int32, (PAD, GRP), 0)
    dense = jnp.zeros((PAD, GRP), f32)
    for k in range(ids.shape[0]):
        dense += jnp.where(lax.rem(row, 16) == ids[k:k + 1], share[k:k + 1], 0.0)
    dense = jnp.transpose(dense)
    lanes = lax.broadcasted_iota(jnp.int32, (ROWS, PAD), 1)
    tile = jnp.zeros((ROWS, PAD), f32)
    for c in range(chunks):
        tile += jnp.where(lax.div(lanes, 16) == c, dense[c * ROWS:(c + 1) * ROWS], 0.0)
    top = tile.astype(bf16)
    held[t, 0, 0, z, 0, :, pl.ds(half, PAD)] = top
    held[t, 0, 0, z, 0, :, pl.ds(half + PAD, PAD)] = (tile - top.astype(f32)).astype(bf16)
    marks[...] = jnp.transpose(jnp.broadcast_to(seq[...].astype(f32), (GRP, PAD)))
    load_tok.wait()
    pl.semaphore_wait(barrier, 5)

    ag_runs = runs([(kind, c == 0) for c, kind in enumerate(AG)])
    rs_runs = runs(RS)

    def ga(c):
        return run_of([(kind, i == 0) for i, kind in enumerate(AG)], c)

    def gr(c):
        return run_of(RS, c)

    def wide(c):
        return pl.ds(0, half + EXTRA) if c == 0 else feats

    def group(c, d, f):
        return held.at[t, c, 0, d, f, :, wide(c)]

    def pair(c, d):
        if AG[c] == "A":
            return group(c, d, 0)
        if AG[c] == "B":
            return held.at[t, c, :, d, :, :, wide(c)]
        return held.at[t, c, 0, d, :, :, wide(c)]

    def near_go(c, d):
        remote(group(c, d, 0), group(c, d, 1), af_s.at[ga(c)], af_r.at[c, d], near).start()

    def fgo(c):
        near_go(c, z)

    def up_go(c, k):
        remote(pair(c, z - k), pair(c, z - k), au_s.at[ga(c)], au_r.at[c, k], above).start()

    def down_go(c, k):
        remote(pair(c, z + k), pair(c, z + k), ad_s.at[ga(c)], ad_r.at[c, k], below).start()

    def far_go(c, d):
        if AG[c] == "A":
            arrived(group(c, d, 1), af_r.at[c, d])
        remote(
            held.at[t, c, 0, d, :, :, wide(c)], held.at[t, c, 1, d, :, :, wide(c)],
            as_s.at[ga(c)], as_r.at[c, d], far,
        ).start()

    def twin_go(c, s):
        for f in range(2):
            remote(
                held.at[t, c, s, :, f, :, feats], held.at[t, c, f, :, s, :, feats],
                at_s.at[0], at_r.at[c], twin,
            ).start()

    def line_go(c):
        pl.when(z < 3)(lambda: up_go(c, 0))
        pl.when(z > 0)(lambda: down_go(c, 0))

    def own(c):
        if AG[c] != "A":
            arrived(group(c, z, 1), af_r.at[c, z])
        if AG[c] != "B":
            line_go(c)
        if AG[c] != "A":
            far_go(c, z)

    def hop(k, c):
        onward = {"A": near_go, "B": None, "C": far_go}[AG[c]]
        last = k == (3 if AG[c] == "C" else 4)
        if AG[c] == "B":
            k -= 1

        def from_below():
            arrived(pair(c, z - k), au_r.at[c, k - 1])
            if k < 3:
                pl.when(z < 3)(lambda: up_go(c, k))
            if onward:
                onward(c, z - k)

        def from_above():
            arrived(pair(c, z + k), ad_r.at[c, k - 1])
            if k < 3:
                pl.when(z > 0)(lambda: down_go(c, k))
            if onward:
                onward(c, z + k)

        if k == 0:
            arrived(held.at[t, c, 1, z, :, :, wide(c)], as_r.at[c, z])
            line_go(c)
        elif k < 4:
            pl.when(z >= k)(from_below)
            pl.when(z + k <= 3)(from_above)
        if AG[c] == "A":
            if k == 1:
                far_go(c, z)
            else:
                pl.when(z >= k - 1)(lambda: far_go(c, z - (k - 1)))
                pl.when(z + k - 1 <= 3)(lambda: far_go(c, z + k - 1))
        if last:
            twin_go(c, 0)
            if AG[c] == "B":
                twin_go(c, 1)

    def sar(c):
        if AG[c] == "B":
            return
        for d in range(4):
            arrived(held.at[t, c, 1, d, :, :, wide(c)], as_r.at[c, d])
        twin_go(c, 1)

    def flat(value):
        return value.reshape(block, value.shape[-1])

    def hidden(c):
        if c == 0:
            for load in loads:
                load.wait()
        arrived(held.at[1 - t, c, :, :, :, :, feats], at_r.at[c])
        lanes = lax.broadcasted_iota(jnp.int32, (block, PAD), 1)
        shares = flat(held[t, 0, :, :, :, :, pl.ds(half, PAD)]).astype(f32)
        shares += flat(held[t, 0, :, :, :, :, pl.ds(half + PAD, PAD)]).astype(f32)
        scale[...] = jnp.sum(jnp.where(lanes == c * 16 + e, shares, 0.0), axis=1, keepdims=True)
        a = flat(held[0, c, :, :, :, :, feats])
        b = flat(held[1, c, :, :, :, :, feats])
        g = jnp.dot(a, gate_w[pl.ds(0, half)], preferred_element_type=f32)
        g += jnp.dot(b, gate_w[pl.ds(half, half)], preferred_element_type=f32)
        u = jnp.dot(a, up_w[pl.ds(0, half)], preferred_element_type=f32)
        u += jnp.dot(b, up_w[pl.ds(half, half)], preferred_element_type=f32)
        hid[...] = (g / (1.0 + jnp.exp(-g)) * u * scale[...]).astype(bf16)

    def term(n, core):
        cols = pl.ds(pl.multiple_of(core * half + n * 512, 512), 512)
        return jnp.dot(hid[...], down_w[:, cols], preferred_element_type=f32)

    def other(c):
        def step(n, carry):
            cols = pl.ds(pl.multiple_of(n * 512, 512), 512)
            value = term(n, 1 - t).astype(bf16)
            held[1 - t, c, :, :, :, :, cols] = value.reshape(2, 4, 2, ROWS, 512)
            return carry

        lax.fori_loop(0, half // 512, step, 0)
        for s in range(2):
            for f in range(2):
                remote(
                    held.at[1 - t, c, s, :, f, :, feats], part.at[c, f, :, s],
                    sw_s.at[0], sw_r.at[c], twin,
                ).start()

    def mine(c):
        def step(n, carry):
            cols = pl.ds(pl.multiple_of(n * 512, 512), 512)
            value = term(n, t).astype(bf16)
            own_part[:, :, :, :, cols] = value.reshape(2, 4, 2, ROWS, 512)
            return carry

        lax.fori_loop(0, half // 512, step, 0)
        arrived(part.at[c], sw_r.at[c])
        for d in ORDER:
            add(part.at[c, 1, d], own_part.at[1, d])
            if RS[c] != "B":
                cross(c, d)
        for d in ORDER:
            add(part.at[c, 0, d], own_part.at[0, d])

    def cross(c, d):
        remote(part.at[c, 1, d], s_in.at[c, d], rs_s.at[gr(c)], rs_r.at[c, d], far).start()

    def add(dst, src):
        if len(dst.shape) > 2:
            for f in range(2):
                add(dst.at[f], src.at[f])
        else:
            dst[...] = dst[...] + src[...]

    def ra(c):
        if RS[c] == "B":
            return
        for d in ORDER:
            arrived(s_in.at[c, d], rs_r.at[c, d])
            if RS[c] == "A":
                add(part.at[c, 0, d, 1], s_in.at[c, d, 1])
                remote(
                    part.at[c, 0, d, 1], x_in.at[LAST.index(c), d], rf_s.at[gr(c)], rf_r.at[c, d], near
                ).start()
                add(part.at[c, 0, d, 0], s_in.at[c, d, 0])
            else:
                add(part.at[c, 0, d], s_in.at[c, d])

    def fa(c):
        if RS[c] == "A":
            for d in ORDER:
                arrived(x_in.at[LAST.index(c), d], rf_r.at[c, d])
                add(part.at[c, 0, d, 0], x_in.at[LAST.index(c), d])

    def line_ref(c, d):
        if RS[c] == "B":
            return part.at[c, :, d]
        return part.at[c, 0, d, 0] if RS[c] == "A" else part.at[c, 0, d]

    def came_ref(way, c, slot):
        if RS[c] == "B":
            return q_in.at[way, QUADS.index(c), slot]
        ref = (u_in, d_in)[way]
        return ref.at[c, slot, 0] if RS[c] == "A" else ref.at[c, slot]

    def join(way, c, d, slot):
        arrived(came_ref(way, c, slot), (ru_r, rd_r)[way].at[c, slot])
        add(line_ref(c, d), came_ref(way, c, slot))

    def cs(h, c):
        def up():
            for d in range(3, h, -1):
                if h > 0:
                    join(0, c, d, d - 1)
                remote(
                    line_ref(c, d), came_ref(0, c, d - 1),
                    ru_s.at[gr(c)], ru_r.at[c, d - 1], above,
                ).start()

        def down():
            for d in range(3 - h):
                if h > 0:
                    join(1, c, d, d)
                remote(
                    line_ref(c, d), came_ref(1, c, d),
                    rd_s.at[gr(c)], rd_r.at[c, d], below,
                ).start()

        pl.when(z == h)(up)
        pl.when(z == 3 - h)(down)

    def end(c):
        pl.when(z > 0)(lambda: join(0, c, z, z - 1))
        pl.when(z < 3)(lambda: join(1, c, z, z))
        if RS[c] == "C":
            hand(c)
        if RS[c] == "B":
            cross(c, z)

    def hand(c):
        remote(part.at[c, 0, z, 1], f_in.at[c], rf_s.at[gr(c)], rf_r.at[c, z], near).start()

    def e2(c):
        if RS[c] == "B":
            arrived(s_in.at[c, z], rs_r.at[c, z])
            add(part.at[c, 0, z, 1], s_in.at[c, z, 1])
            hand(c)
            add(part.at[c, 0, z, 0], s_in.at[c, z, 0])

    def fin(c):
        total = part[c, 0, z, 0].astype(f32)
        if RS[c] != "A":
            arrived(f_in.at[c], rf_r.at[c, z])
            total += f_in[c].astype(f32)
        total += held[t, c, 0, z, 0, :, feats].astype(f32)
        rounded = total.astype(bf16)
        rows = pl.ds(c * ROWS, ROWS)
        stage[rows] = rounded
        pltpu.make_async_copy(stage.at[rows], out.at[rows], out_sem).start()
        as_float = rounded.astype(f32)
        squares = jnp.sum(as_float * as_float, axis=1, keepdims=True)
        along = jnp.sum(as_float * value_row[...], axis=1, keepdims=True)
        lanes = lax.broadcasted_iota(jnp.int32, (ROWS, PAD), 1)
        stats[0, rows] = jnp.where(lanes == 0, squares, along)

    steps = {
        "fgo": fgo, "own": own, "sar": sar, "hid": hidden, "oth": other, "mine": mine, "ra": ra,
        "fa": fa, "end": end, "e2": e2, "fin": fin,
    }
    for k in range(1, 5):
        steps["hop%d" % k] = functools.partial(hop, k)
        steps["cs%d" % (k - 1)] = functools.partial(cs, k - 1)
    turns = [(place, 0, c, name) for name, places in PLAN for c, place in enumerate(places) if place is not None]
    for _, _, c, name in sorted(turns):
        steps[name](c)

    trade = remote(stats.at[0], stats.at[1], v_sem.at[0], v_sem.at[1], twin)
    trade.start()
    left(held.at[t, :, :, :, :, :, feats], at_s.at[0])
    left(part, sw_s.at[0])
    for i, (first, stop) in enumerate(ag_runs):
        run, w = pl.ds(first, stop - first), wide(first)
        single = AG[first] == "A"
        left(held.at[t, run, 0, pl.ds(0, 4 if single else 1), 0, :, w], af_s.at[i])
        left(held.at[t, run, 0, pl.ds(0, 1 if AG[first] == "B" else 4), :, :, w], as_s.at[i])
    for i, (first, stop) in enumerate(rs_runs):
        run = pl.ds(first, stop - first)
        left(part.at[run, 0, pl.ds(0, 4 if RS[first] == "A" else 1), 0], rf_s.at[i])
        left(part.at[run, 1, pl.ds(0, 1 if RS[first] == "B" else 4)], rs_s.at[i])

    def line_sent(k):
        for i, (first, stop) in enumerate(ag_runs):
            run, w = pl.ds(first, stop - first), wide(first)
            f = pl.ds(0, 1 if AG[first] == "A" else 2)
            r = pl.ds(0, 2 if AG[first] == "B" else 1)
            if k < 3:
                left(held.at[t, run, r, pl.ds(0, k + 1), f, :, w], au_s.at[i])
            if k > 0:
                left(held.at[t, run, r, pl.ds(0, 4 - k), f, :, w], ad_s.at[i])
        for i, (first, stop) in enumerate(rs_runs):
            run = pl.ds(first, stop - first)
            f = pl.ds(0, 1 if RS[first] == "A" else 2)
            r = pl.ds(0, 2 if RS[first] == "B" else 1)
            if k < 3:
                left(part.at[run, r, pl.ds(0, 3 - k), f], ru_s.at[i])
            if k > 0:
                left(part.at[run, r, pl.ds(0, k), f], rd_s.at[i])

    for k in range(4):
        pl.when(z == k)(functools.partial(line_sent, k))
    pltpu.make_async_copy(stage, out, out_sem).wait()
    trade.wait()
    both = stats[0] + stats[1]
    values = both[:, 1:2] * lax.rsqrt(both[:, 0:1] / (2 * half) + 1e-06)
    lane = lax.broadcasted_iota(jnp.int32, (GRP, PAD), 1)
    members = (marks[...] == lane.astype(f32)).astype(f32)
    sums = jnp.sum(members * values, axis=0, keepdims=True)
    counts = jnp.sum(members, axis=0, keepdims=True)
    rewards[...] = (sums / jnp.maximum(counts, 1.0))[:, :SEQ_GRP]


def routed_layer(tokens, ids, weights, value_row, seq, gate, up, down):
    chunks, rows, half = tokens.shape
    width, units = gate.shape
    bf16 = jnp.bfloat16
    dma = pltpu.SemaphoreType.DMA
    flops = 2 * 16 * GRP * 3 * width * units
    vmem, anywhere = pl.BlockSpec(memory_space=pltpu.VMEM), pl.BlockSpec(memory_space=pl.ANY)
    return pl.pallas_call(
        fused,
        out_shape=(
            jax.ShapeDtypeStruct((GRP, half), bf16),
            jax.ShapeDtypeStruct((1, SEQ_GRP), jnp.float32),
        ),
        in_specs=[anywhere] + [vmem] * 4 + [anywhere] * 3,
        out_specs=(anywhere, vmem),
        scratch_shapes=[
            pltpu.VMEM((2, chunks, 2, 4, 2, rows, half + EXTRA), bf16),
            pltpu.VMEM((width, units), bf16),
            pltpu.VMEM((width, units), bf16),
            pltpu.VMEM((units, width), bf16),
            pltpu.VMEM((16 * rows, units), bf16),
            pltpu.VMEM((16 * rows, 1), jnp.float32),
            pltpu.VMEM((2, 4, 2, rows, half), bf16),
            pltpu.VMEM((chunks, 2, 4, 2, rows, half), bf16),
            pltpu.VMEM((chunks, 4, 2, rows, half), bf16),
            pltpu.VMEM((chunks, 3, 2, rows, half), bf16),
            pltpu.VMEM((chunks, 3, 2, rows, half), bf16),
            pltpu.VMEM((chunks, rows, half), bf16),
            pltpu.VMEM((max(1, len(LAST)), 4, rows, half), bf16),
            pltpu.VMEM((2, max(1, len(QUADS)), 3, 2, 2, rows, half), bf16),
            pltpu.VMEM((2, GRP, PAD), jnp.float32),
            pltpu.VMEM((GRP, PAD), jnp.float32),
            pltpu.VMEM((GRP, half), bf16),
            dma((3,)), dma, dma,
            dma((chunks,)), dma((chunks, 4)),
            dma((chunks,)), dma((chunks, 3)),
            dma((chunks,)), dma((chunks, 3)),
            dma((chunks,)), dma((chunks, 4)),
            dma((1,)), dma((chunks,)),
            dma((1,)), dma((chunks,)),
            dma((chunks,)), dma((chunks, 4)),
            dma((chunks,)), dma((chunks, 3)),
            dma((chunks,)), dma((chunks, 3)),
            dma((chunks,)), dma((chunks, 4)),
            dma((2,)),
        ],
        compiler_params=pltpu.CompilerParams(
            collective_id=0, has_side_effects=True, vmem_limit_bytes=63 * 1024 * 1024
        ),
        cost_estimate=pl.CostEstimate(
            flops=flops, bytes_accessed=6 * width * units, transcendentals=16 * GRP * units
        ),
    )(tokens, ids, weights, value_row, seq, gate, up, down)


def shards(
    tokens,
    expert_ids,
    route_weights,
    gate_weight,
    up_weight,
    down_weight,
    value_weight,
    sequence_ids,
):
    tok_count, width_part = tokens.shape
    return routed_layer(
        tokens.reshape(tok_count // ROWS, ROWS, width_part), expert_ids.T, route_weights.T,
        value_weight[None, :], sequence_ids, gate_weight[0], up_weight[0], down_weight[0],
    )


def solution(mesh):
    in_specs = (
        P("ep", "tp"),
        P("ep", None),
        P("ep", None),
        P("ep", None, "tp"),
        P("ep", None, "tp"),
        P("ep", "tp", None),
        P("tp"),
        P("ep", None),
    )
    out_specs = (P("ep", "tp"), P("ep", None))
    body = shards if dict(mesh.shape) == {"tp": 2, "ep": 16} else plain_shards
    return jax.shard_map(body, mesh=mesh, in_specs=in_specs, out_specs=out_specs, check_vma=False)
```
